256 devices in a mesh: gx: 16 (over z, core), gy: 16 (over y, x).
Axes of the slice: x: 4, y: 4, z: 8, core: 2. Of those that a mesh axis runs over, the one named last changes fastest.
Arguments:
- vapor_ratio: float32 [64, 64, 512], P('gy', 'gx'), may hold values from 0.5 to 1.5
- potential_temp: float32 [64, 64, 512], P('gy', 'gx'), may hold values from -4 to 4
- flow_x: float32 [64, 64, 512], P('gy', 'gx'), may hold values from -0.45 to 0.45
- flow_y: float32 [64, 64, 512], P('gy', 'gx'), may hold values from -0.45 to 0.45
- sat_ref: float32 [32], replicated, may hold values from 0.6 to 1.4
- fall_rate: float32 [32], replicated, may hold values from 0.5 to 4
- drop_mass: float32 [16, 16, 256, 128], P('gx', 'gy'), may hold values from 0.2 to 1.5
- drop_weight: float32 [16, 16, 256, 128], P('gx', 'gy'), may hold values from 0.05 to 0.3
- drop_cells: int32 [16, 16, 256, 128], P('gx', 'gy'), may hold values from 0 to 4095
- drop_counts: int32 [16, 16, 256], P('gx', 'gy'), may hold values from 0 to 128, as said below
- leave_mass: float32 [16, 16, 8, 16, 128], P('gx', 'gy'), may hold values from 0.2 to 1.5
- leave_weight: float32 [16, 16, 8, 16, 128], P('gx', 'gy'), may hold values from 0.05 to 0.3
- leave_cells: int32 [16, 16, 8, 16, 128], P('gx', 'gy'), may hold values from 0 to 4095
- leave_counts: int32 [16, 16, 8, 16], P('gx', 'gy'), may hold values from 0 to 128
Outputs:
- vapor_next: float32 [64, 64, 512], P(None, 'gx', 'gy')
- heat_next: float32 [64, 64, 512], P(None, 'gx', 'gy')
- rain_water: float32 [32, 64, 512], P(None, 'gx', 'gy')
- grown_mass: float32 [16, 16, 384, 128], P('gx', 'gy')
The draws below stay inside these ranges and needn't reach their ends.
Inputs may be any that keep to these rules, and one draw needn't show every extreme that they name: `drop_counts`: each device draws its own ceiling for its resident blocks' counts.
All inputs are finite; a program needn't handle non-finite values.
Results may differ from the reference program's by a relative error of at most 0.0003.
Values sent between devices are 32-bit elements; how exact they have to be, the bound alone decides.
A program may use at most 64 MiB of HBM per device.

```python
import math
import jax
import jax.numpy as jnp
from jax import lax

CX = 4
CY = 32
NZ = 64
CL = 32
BLOCK = 128
MB = 16
NX = 64
NY = 512
CELLS = 4096
RB = 256
N_GX = 16
N_GY = 16


def draw_drop_counts(key, part):
    first_key, second_key = jax.random.split(key)
    ceiling = jax.random.randint(first_key, (N_GX, N_GY, 1), 64, 321)
    drawn = jax.random.randint(second_key, (N_GX, N_GY, RB), 0, 1 << 20)
    return jnp.minimum(drawn % ceiling, BLOCK).astype(jnp.int32)


def place_ends(result, own_key, least, largest):
    longest = result.shape.index(max(result.shape))
    spots = []
    for shift in (0, 1):
        where = [jax.random.randint(jax.random.fold_in(own_key, axis), (), 0, length) for axis, length in enumerate(result.shape)]
        where[longest] = (where[longest] + shift) % result.shape[longest]
        spots.append(tuple(where))
    return result.at[spots[0]].set(least).at[spots[1]].set(largest)


def shard_levels(own_key, extent, cuts, smallest, largest):
    level, own = 1.0, jax.random.fold_in(own_key, 6)
    for dim, blocks in cuts:
        heights = jnp.exp(jax.random.uniform(jax.random.fold_in(own, dim), (blocks,), jnp.float32, smallest / len(cuts), largest / len(cuts)))
        level = level * jnp.repeat(heights, extent[dim] // blocks).reshape([-1 if axis == dim else 1 for axis in range(len(extent))])
    return level


def centred(key, shape, scale, reach, pieces=(), kind=jnp.bfloat16):
    factor_of = shard_levels(key, shape, pieces, -0.22, 0.18) if pieces else 1.0
    values = jax.random.normal(key, shape, jnp.float32) * scale * factor_of
    return jnp.minimum(jnp.maximum(values, -reach), reach).astype(kind)


def setup_inputs(seed: int = 0) -> dict:
    splits = jax.random.split(jax.random.key(seed), 15)
    vapor_ratio = jnp.clip(0.5 + 1.0 * jax.random.uniform(splits[0], (NZ, NX, NY), jnp.float32) ** shard_levels(splits[0], (NZ, NX, NY), ((0, 16), (1, 16)), -0.2, 0.2), 0.5, 1.5)
    potential_temp = centred(splits[1], (NZ, NX, NY), 1.0, 4.0, ((0, 16), (1, 16)), jnp.float32)
    flow_x = jnp.clip(jax.random.uniform(splits[2], (NZ, NX, NY), jnp.float32, -0.45, 0.45) * shard_levels(splits[2], (NZ, NX, NY), ((0, 16), (1, 16)), -0.4, 0.0), -0.45, 0.45)
    flow_y = jnp.clip(jax.random.uniform(splits[3], (NZ, NX, NY), jnp.float32, -0.45, 0.45) * shard_levels(splits[3], (NZ, NX, NY), ((0, 16), (1, 16)), -0.4, 0.0), -0.45, 0.45)
    sat_ref = jnp.clip(jax.random.uniform(splits[4], (CL,), jnp.float32, 0.6, 1.4), 0.6, 1.4)
    fall_rate = jnp.clip(jnp.exp(jax.random.uniform(splits[5], (CL,), jnp.float32, math.log(0.5), math.log(4.0))), 0.5, 4.0)
    drop_mass = jnp.clip(0.2 + 1.3 * jax.random.uniform(splits[6], (N_GX, N_GY, RB, BLOCK), jnp.float32) ** shard_levels(splits[6], (N_GX, N_GY, RB, BLOCK), ((0, 16), (1, 16)), -0.2, 0.2), 0.2, 1.5)
    drop_weight = jnp.clip(0.05 + 0.25 * jax.random.uniform(splits[7], (N_GX, N_GY, RB, BLOCK), jnp.float32) ** shard_levels(splits[7], (N_GX, N_GY, RB, BLOCK), ((0, 16), (1, 16)), -0.2, 0.2), 0.05, 0.3)
    drop_cells = place_ends(jax.random.randint(splits[8], (N_GX, N_GY, RB, BLOCK), 0, CELLS), jax.random.fold_in(splits[8], 1), 0, CELLS - 1).astype(jnp.int32)
    drop_counts = draw_drop_counts(jax.random.fold_in(splits[14], 71), 0)
    leave_mass = jnp.clip(0.2 + 1.3 * jax.random.uniform(splits[10], (N_GX, N_GY, 8, MB, BLOCK), jnp.float32) ** shard_levels(splits[10], (N_GX, N_GY, 8, MB, BLOCK), ((0, 16), (1, 16)), -0.2, 0.2), 0.2, 1.5)
    leave_weight = jnp.clip(0.05 + 0.25 * jax.random.uniform(splits[11], (N_GX, N_GY, 8, MB, BLOCK), jnp.float32) ** shard_levels(splits[11], (N_GX, N_GY, 8, MB, BLOCK), ((0, 16), (1, 16)), -0.2, 0.2), 0.05, 0.3)
    leave_cells = place_ends(jax.random.randint(splits[12], (N_GX, N_GY, 8, MB, BLOCK), 0, CELLS), jax.random.fold_in(splits[12], 1), 0, CELLS - 1).astype(jnp.int32)
    leave_counts = place_ends(jax.random.randint(splits[13], (N_GX, N_GY, 8, MB), 0, BLOCK + 1), jax.random.fold_in(splits[13], 1), 0, BLOCK).astype(jnp.int32)
    return {"vapor_ratio": vapor_ratio, "potential_temp": potential_temp, "flow_x": flow_x, "flow_y": flow_y, "sat_ref": sat_ref, "fall_rate": fall_rate, "drop_mass": drop_mass, "drop_weight": drop_weight, "drop_cells": drop_cells, "drop_counts": drop_counts, "leave_mass": leave_mass, "leave_weight": leave_weight, "leave_cells": leave_cells, "leave_counts": leave_counts}


sat_slope = 0.3
grow_rate = 0.5
latent_heat = 2.5
DIRECTIONS = ((-1, -1), (-1, 0), (-1, 1), (0, -1), (0, 1), (1, -1), (1, 0), (1, 1))


def settle_matrix(fall_rate):
    levels = fall_rate.shape[0]
    keeping = 1.0 / (1.0 + fall_rate)
    passing = jnp.cumsum(jnp.log(fall_rate * keeping))
    upper = jnp.arange(levels, dtype=jnp.int32)[None, :] >= jnp.arange(levels, dtype=jnp.int32)[:, None]
    spread = jnp.where(upper, passing[None, :] - passing[:, None], 0.0)
    return jnp.where(upper, keeping[:, None] * jnp.exp(spread), 0.0)


def advect_periodic(scalar, flow_x, flow_y):
    flux_x = jnp.where(flow_x > 0, flow_x * scalar, flow_x * jnp.roll(scalar, -1, axis=1))
    flux_y = jnp.where(flow_y > 0, flow_y * scalar, flow_y * jnp.roll(scalar, -1, axis=2))
    return scalar - (flux_x - jnp.roll(flux_x, 1, axis=1)) - (flux_y - jnp.roll(flux_y, 1, axis=2))


def one_device(masses, weights, cell_ids, excess_row):
    grown = masses * jnp.exp(grow_rate * excess_row[cell_ids])
    liquid = jax.ops.segment_sum((weights * grown).reshape(-1), cell_ids.reshape(-1), num_segments=excess_row.shape[0])
    condensed = jax.ops.segment_sum((weights * (grown - masses)).reshape(-1), cell_ids.reshape(-1), num_segments=excess_row.shape[0])
    return grown, liquid, condensed


def one_row(packed):
    return jax.vmap(one_device)(*packed)


def reference(vapor_ratio, potential_temp, flow_x, flow_y, sat_ref, fall_rate, drop_mass, drop_weight, drop_cells, drop_counts, leave_mass, leave_weight, leave_cells, leave_counts):
    moisture = advect_periodic(vapor_ratio, flow_x, flow_y)
    warmth = advect_periodic(potential_temp, flow_x, flow_y)
    excess = moisture[:CL] - sat_ref[:, None, None] * jnp.exp(sat_slope * warmth[:CL])
    per_device = excess.reshape(CL, N_GX, CX, N_GY, CY).transpose(1, 3, 0, 2, 4).reshape(N_GX, N_GY, CL * CX * CY)
    lane_ids = jnp.arange(BLOCK, dtype=jnp.int32)
    validity = (lane_ids < drop_counts[..., None]).astype(jnp.float32)
    arrivals = []
    for which, (step_x, step_y) in enumerate(DIRECTIONS):
        moved = (leave_mass[:, :, which], leave_weight[:, :, which], leave_cells[:, :, which], leave_counts[:, :, which])
        arrivals.append(tuple(jnp.roll(piece, (step_x, step_y), axis=(0, 1)) for piece in moved))
    in_mass = jnp.stack([entry[0] for entry in arrivals], axis=2)
    in_weight = jnp.stack([entry[1] for entry in arrivals], axis=2)
    in_cells = jnp.stack([entry[2] for entry in arrivals], axis=2)
    in_counts = jnp.stack([entry[3] for entry in arrivals], axis=2)
    in_valid = (lane_ids < in_counts[..., None]).astype(jnp.float32)
    moving = 8 * MB
    masses = jnp.concatenate([drop_mass * validity, (in_mass * in_valid).reshape(N_GX, N_GY, moving, BLOCK)], axis=2)
    weights = jnp.concatenate([drop_weight * validity, (in_weight * in_valid).reshape(N_GX, N_GY, moving, BLOCK)], axis=2)
    cell_ids = jnp.concatenate([drop_cells, in_cells.reshape(N_GX, N_GY, moving, BLOCK)], axis=2).astype(jnp.int32)
    grown_mass, liquid, condensed = lax.map(one_row, (masses, weights, cell_ids, per_device))
    liquid_grid = liquid.reshape(N_GX, N_GY, CL, CX, CY).transpose(2, 0, 3, 1, 4).reshape(CL, NX, NY)
    cond_grid = condensed.reshape(N_GX, N_GY, CL, CX, CY).transpose(2, 0, 3, 1, 4).reshape(CL, NX, NY)
    vapor_next = jnp.concatenate([moisture[:CL] - cond_grid, moisture[CL:]], axis=0)
    heat_next = jnp.concatenate([warmth[:CL] + latent_heat * cond_grid, warmth[CL:]], axis=0)
    inverse = settle_matrix(fall_rate)
    rain_water = jnp.dot(inverse, liquid_grid.reshape(CL, NX * NY), precision=lax.Precision.HIGHEST, preferred_element_type=jnp.float32).reshape(CL, NX, NY)
    return vapor_next, heat_next, rain_water, grown_mass
```

```python
import functools

import jax
import jax.numpy as jnp
from jax import lax
from jax.experimental import pallas as pl
from jax.experimental.pallas import tpu as pltpu
from jax.sharding import PartitionSpec as P

LANES = 128


def bin_rows(acc, first, last, p_of, c_of, levels, group, unroll):
    one = jnp.ones((), jnp.bfloat16)
    zero = jnp.zeros((), jnp.bfloat16)
    col_iota = lax.broadcasted_iota(jnp.int32, (LANES, LANES), 0).astype(jnp.float32).astype(jnp.bfloat16)
    lev_iota = lax.broadcasted_iota(jnp.int32, (levels, LANES), 0).astype(jnp.float32).astype(jnp.bfloat16)

    def half(j):
        p = p_of(j)
        c = c_of(j)
        hi = p.astype(jnp.bfloat16)
        lo = (p - hi.astype(jnp.float32)).astype(jnp.bfloat16)
        lev = (c >> 7).astype(jnp.float32)
        col = (c & 127).astype(jnp.float32)
        lev = jnp.broadcast_to(lev, (levels, LANES)).astype(jnp.bfloat16)
        col = jnp.broadcast_to(col, (LANES, LANES)).astype(jnp.bfloat16)
        hib = jnp.broadcast_to(hi.astype(jnp.float32), (levels, LANES)).astype(jnp.bfloat16)
        lob = jnp.broadcast_to(lo.astype(jnp.float32), (levels, LANES)).astype(jnp.bfloat16)
        here = lev == lev_iota
        a = jnp.concatenate([jnp.where(here, hib, zero), jnp.where(here, lob, zero)], axis=0)
        b = jnp.where(col == col_iota, one, zero)
        return a, b

    def step(i, acc):
        parts = [half(first + group * i + k) for k in range(group)]
        a = jnp.concatenate([q[0] for q in parts], axis=1)
        b = jnp.concatenate([q[1] for q in parts], axis=1)
        return acc + lax.dot_general(a, b, (((1,), (1,)), ((), ())), preferred_element_type=jnp.float32)

    return lax.fori_loop(0, (last - first) // group, step, acc, unroll=unroll)


def bin_kernel(levels, group, unroll, mass_ref, weight_ref, cells_ref, out_ref, p_ref):
    rows = mass_ref.shape[0]
    p_ref[...] = mass_ref[...] * weight_ref[...]
    acc = jnp.zeros((2 * levels, LANES), jnp.float32)
    acc = bin_rows(acc, 0, rows, lambda j: p_ref[pl.ds(j, 1), :], lambda j: cells_ref[pl.ds(j, 1), :], levels, group, unroll)
    out_ref[...] = acc[:levels] + acc[levels:]


def bin_call(mass, weight, cells, levels, group=8, unroll=1):
    return pl.pallas_call(
        functools.partial(bin_kernel, levels, group, unroll),
        out_shape=jax.ShapeDtypeStruct((levels, LANES), jnp.float32),
        scratch_shapes=[pltpu.VMEM(mass.shape, jnp.float32)],
        name="bin_records",
    )(mass, weight, cells)


def column_of(row):
    n = row.shape[1]
    i = lax.broadcasted_iota(jnp.int32, (n, n), 0)
    j = lax.broadcasted_iota(jnp.int32, (n, n), 1)
    return jnp.sum(jnp.where(i == j, row, 0.0), axis=1, keepdims=True)


def grow_kernel(levels, fields_ref, sums_ref, mass_ref, cells_ref, sat_ref, fall_ref,
                vapor_ref, heat_ref, rain_ref, grown_ref, table_ref):
    parts = fields_ref.shape[0]
    moist, warm = [], []
    low = lax.broadcasted_iota(jnp.int32, (8, LANES), 0) < 4
    for k in range(0, parts, 2):
        a, b = fields_ref[k], fields_ref[k + 1]
        moist.append(jnp.where(low, a, pltpu.roll(b, 4, 0)))
        warm.append(jnp.where(low, pltpu.roll(a, 4, 0), b))
    moist = jnp.concatenate(moist, axis=0)
    warm = jnp.concatenate(warm, axis=0)
    sat = column_of(sat_ref[...])
    excess = moist[:levels] - sat * jnp.exp(0.3 * warm[:levels])
    growth = jnp.exp(0.5 * excess)
    for k in range(levels):
        table_ref[k] = jnp.broadcast_to(growth[k:k + 1], (8, LANES))

    def tile(t, carry):
        rows = pl.ds(pl.multiple_of(t * 8, 8), 8)
        c = cells_ref[rows, :]
        lev, col = c >> 7, c & 127
        got = jnp.zeros((8, LANES), jnp.float32)
        for k in range(levels):
            g = jnp.take_along_axis(table_ref[k], col, axis=1, mode="promise_in_bounds")
            got = jnp.where(lev == k, g, got)
        grown_ref[rows, :] = mass_ref[rows, :] * got
        return carry

    lax.fori_loop(0, mass_ref.shape[0] // 8, tile, 0, unroll=2)

    sums = sums_ref[...]
    liquid = sums * growth
    condensed = sums * (growth - 1.0)
    fall = fall_ref[...]
    keep = 1.0 / (1.0 + fall)
    logq = jnp.log(fall * keep)
    i = lax.broadcasted_iota(jnp.int32, (levels, levels), 0)
    j = lax.broadcasted_iota(jnp.int32, (levels, levels), 1)
    pass_col = jnp.sum(jnp.where(j <= i, logq, 0.0), axis=1, keepdims=True)
    pass_row = jnp.sum(jnp.where(i <= j, column_of(logq), 0.0), axis=0, keepdims=True)
    spread = jnp.where(j >= i, pass_row - pass_col, 0.0)
    inverse = jnp.where(j >= i, column_of(keep) * jnp.exp(spread), 0.0)
    rain = jnp.dot(inverse, liquid, precision=lax.Precision.HIGHEST, preferred_element_type=jnp.float32)
    for x in range(4):
        rain_ref[:, x, :] = rain[:, 32 * x:32 * x + 32]
    vapor_ref[...] = jnp.concatenate([moist[:levels] - condensed, moist[levels:]], axis=0).T
    heat_ref[...] = jnp.concatenate([warm[:levels] + 2.5 * condensed, warm[levels:]], axis=0).T


def grow_call(fields, sums, mass, cells, sat, fall, levels):
    f32 = jnp.float32
    total = 4 * fields.shape[0]
    return pl.pallas_call(
        functools.partial(grow_kernel, levels),
        out_shape=[
            jax.ShapeDtypeStruct((LANES, total), f32),
            jax.ShapeDtypeStruct((LANES, total), f32),
            jax.ShapeDtypeStruct((levels, 4, 32), f32),
            jax.ShapeDtypeStruct(mass.shape, f32),
        ],
        scratch_shapes=[pltpu.VMEM((levels, 8, LANES), f32)],
        name="grow_records",
    )(fields, sums, mass, cells, sat, fall)


def with_halo(cells, sides, width):
    for axis, dim in sides:
        count = lax.axis_size(axis)
        head = lax.slice_in_dim(cells, 0, width, axis=dim)
        tail = lax.slice_in_dim(cells, cells.shape[dim] - width, cells.shape[dim], axis=dim)
        cells = jnp.concatenate(
            [
                lax.ppermute(tail, axis, [(i, (i + 1) % count) for i in range(count)]),
                cells,
                lax.ppermute(head, axis, [((i + 1) % count, i) for i in range(count)]),
            ],
            axis=dim,
        )
    return cells


def pad_rows(tensor):
    return jnp.concatenate([tensor[..., -1:], tensor, tensor[..., :1]], axis=-1)


def advect_block(padded, flow_xpad, flow_ypad):
    scalar = padded[..., 1:-1, 1:-1]
    face_x = flow_xpad[..., :-1, 1:-1]
    flux_x = jnp.where(face_x > 0, face_x * padded[..., :-1, 1:-1], face_x * padded[..., 1:, 1:-1])
    face_y = flow_ypad[..., 1:-1, :-1]
    flux_y = jnp.where(face_y > 0, face_y * padded[..., 1:-1, :-1], face_y * padded[..., 1:-1, 1:])
    return (
        scalar - (flux_x[..., 1:, :] - flux_x[..., :-1, :]) - (flux_y[..., 1:] - flux_y[..., :-1])
    )


def local(
    vapor_ratio,
    potential_temp,
    flow_x,
    flow_y,
    sat_ref,
    fall_rate,
    drop_mass,
    drop_weight,
    drop_cells,
    drop_counts,
    leave_mass,
    leave_weight,
    leave_cells,
    leave_counts,
):
    stacked = jnp.stack([vapor_ratio, potential_temp, flow_x])
    padded = pad_rows(with_halo(stacked, (("gx", 2),), 1))
    flow_ypad = jnp.pad(pad_rows(flow_y), ((0, 0), (1, 1), (0, 0)))
    moved = advect_block(padded[:2], padded[2], flow_ypad)
    levels_in, width_x = moved.shape[1], moved.shape[2]
    count_y = lax.axis_size("gy")
    width_y = moved.shape[3] // count_y
    packed = moved.reshape(2, levels_in, width_x, count_y, width_y).transpose(3, 0, 1, 2, 4)
    packed = packed.reshape(count_y, 2 * levels_in, width_x * width_y)
    fields = lax.all_to_all(packed, "gy", split_axis=0, concat_axis=0, tiled=True)
    cloud_levels = sat_ref.shape[0]
    slot_count = drop_mass.shape[-1]
    lane_ids = jnp.arange(slot_count, dtype=jnp.int32)
    validity = (lane_ids[None, :] < drop_counts[0, 0][:, None]).astype(jnp.float32)
    out_valid = (lane_ids < leave_counts[0, 0][..., None]).astype(jnp.float32)
    parcel = jnp.stack(
        [
            leave_mass[0, 0] * out_valid,
            leave_weight[0, 0] * out_valid,
            leave_cells[0, 0].astype(jnp.float32),
        ],
        axis=2,
    )
    x_send = jnp.stack([parcel[0:3], parcel[5:8]])
    x_padded = with_halo(x_send, (("gx", 0),), 1)
    from_left = x_padded[0]
    from_right = x_padded[3]
    y_send = jnp.stack(
        [
            jnp.stack([parcel[3], from_left[0], from_right[0]]),
            jnp.stack([parcel[4], from_left[2], from_right[2]]),
        ]
    )
    y_padded = with_halo(y_send, (("gy", 0),), 1)
    from_below = y_padded[0]
    from_above = y_padded[3]
    incoming = jnp.stack(
        [
            from_above[2],
            from_right[1],
            from_below[2],
            from_above[0],
            from_below[0],
            from_above[1],
            from_left[1],
            from_below[1],
        ]
    )
    migrants = incoming.reshape((-1,) + incoming.shape[2:])
    masses = jnp.concatenate([drop_mass[0, 0] * validity, migrants[:, 0]], axis=0)
    weights = jnp.concatenate([drop_weight[0, 0] * validity, migrants[:, 1]], axis=0)
    cell_ids = jnp.concatenate([drop_cells[0, 0], migrants[:, 2].astype(jnp.int32)], axis=0)
    sums = bin_call(masses, weights, cell_ids, cloud_levels, 16, 2)
    vapor, heat, rain_water, grown = grow_call(
        fields, sums, masses, cell_ids, sat_ref[None], fall_rate[None], cloud_levels
    )
    vapor_next = vapor.reshape(width_x, width_y, -1).transpose(2, 0, 1)
    heat_next = heat.reshape(width_x, width_y, -1).transpose(2, 0, 1)
    return (vapor_next, heat_next, rain_water, grown[None, None])


def solution(mesh):
    placed = (
        P("gy", "gx", None),
        P("gy", "gx", None),
        P("gy", "gx", None),
        P("gy", "gx", None),
        P(),
        P(),
        P("gx", "gy", None, None),
        P("gx", "gy", None, None),
        P("gx", "gy", None, None),
        P("gx", "gy", None),
        P("gx", "gy", None, None, None),
        P("gx", "gy", None, None, None),
        P("gx", "gy", None, None, None),
        P("gx", "gy", None, None),
    )
    return jax.shard_map(
        local,
        mesh=mesh,
        in_specs=placed,
        out_specs=(
            P(None, "gx", "gy"),
            P(None, "gx", "gy"),
            P(None, "gx", "gy"),
            P("gx", "gy", None, None),
        ),
        check_vma=False,
    )
```

```python
import functools

import jax
import jax.numpy as jnp
from jax import lax
from jax.experimental import pallas as pl
from jax.experimental.pallas import tpu as pltpu
from jax.sharding import PartitionSpec as P

LANES = 128
PACK = 16
SAT_SLOPE = 0.3
GROW_RATE = 0.5
LATENT_HEAT = 2.5
OFFSETS = ((-1, -1), (-1, 0), (-1, 1), (0, -1), (0, 1), (1, -1), (1, 0), (1, 1))
MESH = pl.DeviceIdType.MESH


def stage_rows(first, rows, mass, weight, cells, limit, hi, lo, lev, col):
    lane = lax.broadcasted_iota(jnp.int32, (8, LANES), 1)

    def tile(t, carry):
        at = pl.ds(pl.multiple_of(first + t * 8, 8), 8)
        m = jnp.where(lane < limit[at, :], mass[at, :], 0.0)
        mass[at, :] = m
        p = m * weight[at, :]
        top = p.astype(jnp.bfloat16).astype(jnp.float32)
        c = cells[at, :]
        hi[at, :] = top
        lo[at, :] = p - top
        lev[at, :] = (c >> 7).astype(jnp.float32)
        col[at, :] = (c & (LANES - 1)).astype(jnp.float32)
        return carry

    lax.fori_loop(0, rows // 8, tile, 0, unroll=4)


def add_rows(acc, first, rows, hi, lo, lev, col, n_lev, group):
    bf16 = jnp.bfloat16
    zero = jnp.zeros((PACK, LANES), bf16)
    one = jnp.ones((PACK, LANES), bf16)
    base = lax.broadcasted_iota(jnp.int32, (PACK, LANES), 0)
    marks = [(base + PACK * g).astype(jnp.float32).astype(bf16) for g in range(LANES // PACK)]

    def step(i, acc):
        left, right = [], []
        for k in range(group):
            j = first + i * group + k

            def spread(ref, j=j):
                return jnp.broadcast_to(ref[pl.ds(j, 1), :], (PACK, LANES)).astype(bf16)

            h, l, v, c = spread(hi), spread(lo), spread(lev), spread(col)
            here = [v == marks[g] for g in range(n_lev)]
            picked = [jnp.where(m, h, zero) for m in here] + [jnp.where(m, l, zero) for m in here]
            right.append(jnp.concatenate(picked, axis=0))
            left.append(jnp.concatenate([jnp.where(c == m, one, zero) for m in marks], axis=0))
        left = jnp.concatenate(left, axis=1)
        right = jnp.concatenate(right, axis=1)
        return acc + lax.dot_general(
            left, right, (((1,), (1,)), ((), ())), preferred_element_type=jnp.float32
        )

    return lax.fori_loop(0, rows // group, step, acc)


def exchange_kernel(
    n_gx, n_gy, levels, cuts,
    vapor, warm, flow_x, flow_y, mass, weight, cells, counts,
    leave_mass, leave_weight, leave_cells, leave_counts,
    fields, all_mass, all_cells, sums,
    scalars, faces_x, faces_y, all_weight, counts_in, slots, limit, hi, lo, lev, col, packed,
    load_sem, drop_sem, halo_send, halo_recv, move_send, move_recv, turn_send, turn_recv,
):
    me_x, me_y = lax.axis_index("gx"), lax.axis_index("gy")

    def at_x(step):
        return lax.rem(me_x + (step + n_gx), n_gx)

    def at_y(step):
        return lax.rem(me_y + (step + n_gy), n_gy)

    resident = mass.shape[2]
    moving = leave_mass.shape[3]
    width_x = vapor.shape[1]
    slab = vapor.shape[0]

    barrier = pltpu.get_barrier_semaphore()
    peers = [(me_x, at_y(o)) for o in range(1, n_gy)]
    peers += [(at_x(dx), at_y(dy)) for dx in (-1, 1) for dy in (-1, 0, 1)]
    for peer in peers:
        pl.semaphore_signal(barrier, inc=1, device_id=peer, device_id_type=MESH)

    drops = [
        pltpu.make_async_copy(counts.at[0], counts_in, drop_sem.at[0]),
        pltpu.make_async_copy(mass.at[0, 0], all_mass.at[pl.ds(0, resident)], drop_sem.at[1]),
        pltpu.make_async_copy(weight.at[0, 0], all_weight.at[pl.ds(0, resident)], drop_sem.at[2]),
        pltpu.make_async_copy(cells.at[0, 0], all_cells.at[pl.ds(0, resident)], drop_sem.at[3]),
    ]
    for copy in drops:
        copy.start()
    loads = []
    for x in range(width_x):
        for source, target in (
            (vapor, scalars.at[x + 1, pl.ds(0, slab)]),
            (warm, scalars.at[x + 1, pl.ds(slab, slab)]),
            (flow_x, faces_x.at[x + 1]),
            (flow_y, faces_y.at[x]),
        ):
            loads.append(pltpu.make_async_copy(source.at[:, x, :], target, load_sem.at[len(loads)]))
    for copy in loads:
        copy.start()

    drops[0].wait()
    for k in range(resident // LANES):
        row = counts_in[:, k * LANES:(k + 1) * LANES]
        turned = jnp.broadcast_to(row, (8, LANES)).T
        limit[k * LANES:(k + 1) * LANES, :] = jnp.broadcast_to(turned[:, 0:1], (LANES, LANES))
    for copy in drops[1:]:
        copy.wait()
    stage_rows(0, resident, all_mass, all_weight, all_cells, limit, hi, lo, lev, col)
    n_lev = -(-levels // PACK)
    acc = jnp.zeros((LANES, 2 * n_lev * PACK), jnp.float32)
    add = functools.partial(add_rows, hi=hi, lo=lo, lev=lev, col=col, n_lev=n_lev, group=16)
    acc = add(acc, 0, cuts[0])

    pl.semaphore_wait(barrier, len(peers))

    halos = []
    for source, x, step, target in (
        (vapor, width_x - 1, 1, scalars.at[0, pl.ds(0, slab)]),
        (warm, width_x - 1, 1, scalars.at[0, pl.ds(slab, slab)]),
        (flow_x, width_x - 1, 1, faces_x.at[0]),
        (vapor, 0, -1, scalars.at[width_x + 1, pl.ds(0, slab)]),
        (warm, 0, -1, scalars.at[width_x + 1, pl.ds(slab, slab)]),
    ):
        k = len(halos)
        halos.append(
            pltpu.make_async_remote_copy(
                src_ref=source.at[:, x, :], dst_ref=target,
                send_sem=halo_send.at[k], recv_sem=halo_recv.at[k],
                device_id=(at_x(step), me_y), device_id_type=MESH,
            )
        )
    for copy in halos:
        copy.start()

    moves = []
    for d, (dx, dy) in enumerate(OFFSETS):
        rows = pl.ds(resident + d * moving, moving)
        for k, (source, target) in enumerate((
            (leave_counts.at[0, 0], slots.at[d]),
            (leave_mass.at[0, 0, d], all_mass.at[rows]),
            (leave_weight.at[0, 0, d], all_weight.at[rows]),
            (leave_cells.at[0, 0, d], all_cells.at[rows]),
        )):
            moves.append(
                pltpu.make_async_remote_copy(
                    src_ref=source, dst_ref=target,
                    send_sem=move_send.at[d, k], recv_sem=move_recv.at[d, k],
                    device_id=(at_x(dx), at_y(dy)), device_id_type=MESH,
                )
            )
    for copy in moves:
        copy.start()
    acc = add(acc, cuts[0], cuts[1] - cuts[0])

    for copy in loads:
        copy.wait()
    for copy in halos:
        copy.wait_recv()
    doubled = lambda face: jnp.concatenate([face, face], axis=0)
    length = scalars.shape[2]
    flux_x = []
    for x in range(width_x + 1):
        face = doubled(faces_x[x])
        flux_x.append(jnp.where(face > 0, face * scalars[x], face * scalars[x + 1]))
    moved = []
    for x in range(width_x):
        here, face = scalars[x + 1], doubled(faces_y[x])
        flux_y = jnp.where(face > 0, face * here, face * pltpu.roll(here, length - 1, 1))
        moved.append(
            here - (flux_x[x + 1] - flux_x[x]) - (flux_y - pltpu.roll(flux_y, 1, 1))
        )

    width_y = LANES // width_x
    block = lax.broadcasted_iota(jnp.int32, (2 * slab, LANES), 1) // width_y
    for k in range(length // LANES):
        rows = [m[:, k * LANES:(k + 1) * LANES] for m in moved]
        for q in range(width_x):
            tile = rows[q]
            for x in range(width_x):
                if x != q:
                    turned = pltpu.roll(rows[x], ((x - q) % width_x) * width_y, 1)
                    tile = jnp.where(block == x, turned, tile)
            packed[k * width_x + q] = tile
    turns = []
    for o in range(1, n_gy):
        peer = at_y(o)
        turns.append(
            pltpu.make_async_remote_copy(
                src_ref=packed.at[peer], dst_ref=fields.at[me_y],
                send_sem=turn_send.at[o], recv_sem=turn_recv.at[o],
                device_id=(me_x, peer), device_id_type=MESH,
            )
        )
    for copy in turns:
        copy.start()
    fields[me_y] = packed[me_y]

    acc = add(acc, cuts[1], resident - cuts[1])
    for copy in moves:
        copy.wait_recv()
    row_of = lax.broadcasted_iota(jnp.int32, slots.shape[1:], 0)
    table = jnp.zeros(slots.shape[1:], jnp.int32)
    for d in range(len(OFFSETS)):
        table = jnp.where(row_of == d, slots[d], table)
    turned = table.T
    for d in range(len(OFFSETS)):
        limit[resident + d * moving:resident + (d + 1) * moving, :] = jnp.broadcast_to(
            turned[:, d:d + 1], (moving, LANES)
        )
    arrived = len(OFFSETS) * moving
    stage_rows(resident, arrived, all_mass, all_weight, all_cells, limit, hi, lo, lev, col)
    acc = add(acc, resident, arrived)
    total = acc.T
    sums[...] = total[:levels] + total[n_lev * PACK:n_lev * PACK + levels]

    for copy in turns:
        copy.wait_recv()
    for copy in halos + moves + turns:
        copy.wait_send()


def exchange_call(n_gx, n_gy, args, levels, cuts):
    vapor, mass, leave = args[0], args[4], args[8]
    slab, width_x, length = vapor.shape
    resident, moving = mass.shape[2], leave.shape[3]
    total = resident + len(OFFSETS) * moving
    f32, i32 = jnp.float32, jnp.int32
    vmem, dma = pltpu.VMEM, pltpu.SemaphoreType.DMA
    record = vmem((total, LANES), f32)
    return pl.pallas_call(
        functools.partial(exchange_kernel, n_gx, n_gy, levels, cuts),
        out_shape=[
            jax.ShapeDtypeStruct((n_gy, 2 * slab, LANES), f32),
            jax.ShapeDtypeStruct((total, LANES), f32),
            jax.ShapeDtypeStruct((total, LANES), i32),
            jax.ShapeDtypeStruct((levels, LANES), f32),
        ],
        in_specs=[pl.BlockSpec(memory_space=pl.ANY)] * len(args),
        out_specs=[pl.BlockSpec(memory_space=vmem)] * 4,
        scratch_shapes=[
            vmem((width_x + 2, 2 * slab, length), f32),
            vmem((width_x + 1, slab, length), f32),
            vmem((width_x, slab, length), f32),
            record,
            vmem((1, resident), i32),
            vmem((len(OFFSETS), len(OFFSETS), moving), i32),
            vmem((total, LANES), i32),
            record, record, record, record,
            vmem((n_gy, 2 * slab, LANES), f32),
            dma((4 * width_x,)), dma((4,)), dma((5,)), dma((5,)),
            dma((len(OFFSETS), 4)), dma((len(OFFSETS), 4)), dma((n_gy,)), dma((n_gy,)),
        ],
        compiler_params=pltpu.CompilerParams(
            collective_id=0, has_side_effects=True, vmem_limit_bytes=16 * 1024 * 1024
        ),
        name="exchange",
    )(*args)


def column_of(row):
    n = row.shape[1]
    i = lax.broadcasted_iota(jnp.int32, (n, n), 0)
    j = lax.broadcasted_iota(jnp.int32, (n, n), 1)
    return jnp.sum(jnp.where(i == j, row, 0.0), axis=1, keepdims=True)


def settle_matrix(fall, levels):
    keep = 1.0 / (1.0 + fall)
    logs = jnp.log(fall * keep)
    i = lax.broadcasted_iota(jnp.int32, (levels, levels), 0)
    j = lax.broadcasted_iota(jnp.int32, (levels, levels), 1)
    down = jnp.sum(jnp.where(j <= i, logs, 0.0), axis=1, keepdims=True)
    across = jnp.sum(jnp.where(i <= j, column_of(logs), 0.0), axis=0, keepdims=True)
    spread = jnp.where(j >= i, across - down, 0.0)
    return jnp.where(j >= i, column_of(keep) * jnp.exp(spread), 0.0)


def grow_kernel(
    levels, unroll, width_x, fields, sums, mass, cells, sat, fall, vapor, heat, rain, grown, table
):
    moist, warm = [], []
    low = lax.broadcasted_iota(jnp.int32, (8, LANES), 0) < 4
    for k in range(0, fields.shape[0], 2):
        a, b = fields[k], fields[k + 1]
        moist.append(jnp.where(low, a, pltpu.roll(b, 4, 0)))
        warm.append(jnp.where(low, pltpu.roll(a, 4, 0), b))
    moist = jnp.concatenate(moist, axis=0)
    warm = jnp.concatenate(warm, axis=0)
    excess = moist[:levels] - column_of(sat[...]) * jnp.exp(SAT_SLOPE * warm[:levels])
    growth = jnp.exp(GROW_RATE * excess)
    for k in range(levels):
        table[k] = jnp.broadcast_to(growth[k:k + 1], (8, LANES))

    def tile(t, carry):
        rows = pl.ds(pl.multiple_of(t * 8, 8), 8)
        c = cells[rows, :]
        lev, col = c >> 7, c & (LANES - 1)
        got = jnp.zeros((8, LANES), jnp.float32)
        for k in range(levels):
            near = jnp.take_along_axis(table[k], col, axis=1, mode="promise_in_bounds")
            got = jnp.where(lev == k, near, got)
        grown[rows, :] = mass[rows, :] * got
        return carry

    lax.fori_loop(0, mass.shape[0] // 8, tile, 0, unroll=unroll)

    total = sums[...]
    liquid = total * growth
    condensed = total * (growth - 1.0)
    fallen = jnp.dot(
        settle_matrix(fall[...], levels), liquid,
        precision=lax.Precision.HIGHEST, preferred_element_type=jnp.float32,
    )
    width_y = LANES // width_x
    for x in range(width_x):
        rain[:, x, :] = fallen[:, x * width_y:(x + 1) * width_y]
    vapor[...] = jnp.concatenate([moist[:levels] - condensed, moist[levels:]], axis=0).T
    heat[...] = jnp.concatenate([warm[:levels] + LATENT_HEAT * condensed, warm[levels:]], axis=0).T


def grow_call(fields, sums, mass, cells, sat, fall, levels, width_x, unroll=16):
    f32 = jnp.float32
    total = fields.shape[0] * fields.shape[1] // 2
    return pl.pallas_call(
        functools.partial(grow_kernel, levels, unroll, width_x),
        out_shape=[
            jax.ShapeDtypeStruct((LANES, total), f32),
            jax.ShapeDtypeStruct((LANES, total), f32),
            jax.ShapeDtypeStruct((levels, width_x, LANES // width_x), f32),
            jax.ShapeDtypeStruct(mass.shape, f32),
        ],
        scratch_shapes=[pltpu.VMEM((levels, 8, LANES), f32)],
        compiler_params=pltpu.CompilerParams(vmem_limit_bytes=16 * 1024 * 1024),
        name="grow_records",
    )(fields, sums, mass, cells, sat, fall)


def local(n_gx, n_gy, vapor_ratio, potential_temp, flow_x, flow_y, sat_ref, fall_rate, *records):
    levels, width_x = sat_ref.shape[0], vapor_ratio.shape[1]
    args = (vapor_ratio, potential_temp, flow_x, flow_y) + records
    resident = records[0].shape[2]
    cuts = (resident * 3 // 8, resident * 6 // 8)
    fields, mass, cells, sums = exchange_call(n_gx, n_gy, args, levels, cuts)
    vapor, heat, rain, grown = grow_call(
        fields, sums, mass, cells, sat_ref[None], fall_rate[None], levels, width_x
    )
    unfold = lambda columns: columns.reshape(width_x, LANES // width_x, -1).transpose(2, 0, 1)
    return unfold(vapor), unfold(heat), rain, grown[None, None]


def solution(mesh):
    level_rows = P("gy", "gx", None)
    owned = lambda rank: P("gx", "gy", *([None] * (rank - 2)))
    return jax.shard_map(
        functools.partial(local, mesh.shape["gx"], mesh.shape["gy"]),
        mesh=mesh,
        in_specs=(level_rows,) * 4 + (P(), P()) + tuple(owned(r) for r in (4, 4, 4, 3, 5, 5, 5, 4)),
        out_specs=(P(None, "gx", "gy"),) * 3 + (owned(4),),
        check_vma=False,
    )
```

```python
import functools

import jax
import jax.numpy as jnp
from jax import lax
from jax.experimental import pallas as pl
from jax.experimental.pallas import tpu as pltpu
from jax.sharding import PartitionSpec as P

LANES = 128
PACK = 16
SAT_SLOPE = 0.3
GROW_RATE = 0.5
LATENT_HEAT = 2.5
OFFSETS = ((-1, -1), (-1, 0), (-1, 1), (0, -1), (0, 1), (1, -1), (1, 0), (1, 1))
MESH = pl.DeviceIdType.MESH


def stage_rows(first, rows, mass, weight, cells, limit, hi, lo, lev, col):
    lane = lax.broadcasted_iota(jnp.int32, (8, LANES), 1)

    def tile(t, carry):
        at = pl.ds(pl.multiple_of(first + t * 8, 8), 8)
        m = jnp.where(lane < limit[at, :], mass[at, :], 0.0)
        mass[at, :] = m
        p = m * weight[at, :]
        top = p.astype(jnp.bfloat16).astype(jnp.float32)
        c = cells[at, :]
        hi[at, :] = top
        lo[at, :] = p - top
        lev[at, :] = (c >> 7).astype(jnp.float32)
        col[at, :] = (c & (LANES - 1)).astype(jnp.float32)
        return carry

    lax.fori_loop(0, rows // 8, tile, 0, unroll=4)


def add_rows(acc, first, rows, hi, lo, lev, col, n_lev, group):
    bf16 = jnp.bfloat16
    zero = jnp.zeros((PACK, LANES), bf16)
    one = jnp.ones((PACK, LANES), bf16)
    base = lax.broadcasted_iota(jnp.int32, (PACK, LANES), 0)
    marks = [(base + PACK * g).astype(jnp.float32).astype(bf16) for g in range(LANES // PACK)]

    def step(i, acc):
        left, right = [], []
        for k in range(group):
            j = first + i * group + k

            def spread(ref, j=j):
                return jnp.broadcast_to(ref[pl.ds(j, 1), :], (PACK, LANES)).astype(bf16)

            h, l, v, c = spread(hi), spread(lo), spread(lev), spread(col)
            here = [v == marks[g] for g in range(n_lev)]
            picked = [jnp.where(m, h, zero) for m in here] + [jnp.where(m, l, zero) for m in here]
            right.append(jnp.concatenate(picked, axis=0))
            left.append(jnp.concatenate([jnp.where(c == m, one, zero) for m in marks], axis=0))
        left = jnp.concatenate(left, axis=1)
        right = jnp.concatenate(right, axis=1)
        return acc + lax.dot_general(
            left, right, (((1,), (1,)), ((), ())), preferred_element_type=jnp.float32
        )

    return lax.fori_loop(0, rows // group, step, acc)


def exchange_kernel(
    n_gx, n_gy, levels, cut,
    vapor, warm, flow_x, flow_y, mass, weight, cells, counts,
    leave_mass, leave_weight, leave_cells, leave_counts,
    fields, all_mass, all_cells, sums,
    scalars, faces_x, faces_y, all_weight, counts_in, slots, limit, hi, lo, lev, col, packed,
    load_sem, drop_sem, halo_send, halo_recv, move_send, move_recv, turn_send, turn_recv,
):
    me_x, me_y = lax.axis_index("gx"), lax.axis_index("gy")

    def at_x(step):
        return lax.rem(me_x + (step + n_gx), n_gx)

    def at_y(step):
        return lax.rem(me_y + (step + n_gy), n_gy)

    resident = mass.shape[2]
    moving = leave_mass.shape[3]
    width_x = vapor.shape[1]
    slab = vapor.shape[0]

    barrier = pltpu.get_barrier_semaphore()
    peers = [(me_x, at_y(o)) for o in range(1, n_gy)]
    peers += [(at_x(dx), at_y(dy)) for dx in (-1, 1) for dy in (-1, 0, 1)]
    for peer in peers:
        pl.semaphore_signal(barrier, inc=1, device_id=peer, device_id_type=MESH)

    drops = [
        pltpu.make_async_copy(counts.at[0], counts_in, drop_sem.at[0]),
        pltpu.make_async_copy(mass.at[0, 0], all_mass.at[pl.ds(0, resident)], drop_sem.at[1]),
        pltpu.make_async_copy(weight.at[0, 0], all_weight.at[pl.ds(0, resident)], drop_sem.at[2]),
        pltpu.make_async_copy(cells.at[0, 0], all_cells.at[pl.ds(0, resident)], drop_sem.at[3]),
    ]
    for copy in drops:
        copy.start()
    loads = []
    for x in range(width_x):
        for source, target in (
            (vapor, scalars.at[x + 1, pl.ds(0, slab)]),
            (warm, scalars.at[x + 1, pl.ds(slab, slab)]),
            (flow_x, faces_x.at[x + 1]),
            (flow_y, faces_y.at[x]),
        ):
            loads.append(pltpu.make_async_copy(source.at[:, x, :], target, load_sem.at[len(loads)]))
    for copy in loads:
        copy.start()

    pl.semaphore_wait(barrier, len(peers))

    halos = []
    for source, x, step, target in (
        (vapor, width_x - 1, 1, scalars.at[0, pl.ds(0, slab)]),
        (warm, width_x - 1, 1, scalars.at[0, pl.ds(slab, slab)]),
        (flow_x, width_x - 1, 1, faces_x.at[0]),
        (vapor, 0, -1, scalars.at[width_x + 1, pl.ds(0, slab)]),
        (warm, 0, -1, scalars.at[width_x + 1, pl.ds(slab, slab)]),
    ):
        k = len(halos)
        halos.append(
            pltpu.make_async_remote_copy(
                src_ref=source.at[:, x, :], dst_ref=target,
                send_sem=halo_send.at[k], recv_sem=halo_recv.at[k],
                device_id=(at_x(step), me_y), device_id_type=MESH,
            )
        )
    for copy in halos:
        copy.start()

    moves = []
    for d, (dx, dy) in enumerate(OFFSETS):
        rows = pl.ds(resident + d * moving, moving)
        for k, (source, target) in enumerate((
            (leave_counts.at[0, 0], slots.at[d]),
            (leave_mass.at[0, 0, d], all_mass.at[rows]),
            (leave_weight.at[0, 0, d], all_weight.at[rows]),
            (leave_cells.at[0, 0, d], all_cells.at[rows]),
        )):
            moves.append(
                pltpu.make_async_remote_copy(
                    src_ref=source, dst_ref=target,
                    send_sem=move_send.at[d, k], recv_sem=move_recv.at[d, k],
                    device_id=(at_x(dx), at_y(dy)), device_id_type=MESH,
                )
            )
    for copy in moves:
        copy.start()
    drops[0].wait()
    for k in range(resident // LANES):
        row = counts_in[:, k * LANES:(k + 1) * LANES]
        turned = jnp.broadcast_to(row, (8, LANES)).T
        limit[k * LANES:(k + 1) * LANES, :] = jnp.broadcast_to(turned[:, 0:1], (LANES, LANES))
    for copy in drops[1:]:
        copy.wait()
    stage_rows(0, resident, all_mass, all_weight, all_cells, limit, hi, lo, lev, col)
    n_lev = -(-levels // PACK)
    acc = jnp.zeros((LANES, 2 * n_lev * PACK), jnp.float32)
    add = functools.partial(add_rows, hi=hi, lo=lo, lev=lev, col=col, n_lev=n_lev, group=16)
    acc = add(acc, 0, cut)

    for copy in loads:
        copy.wait()
    for copy in halos:
        copy.wait_recv()
    doubled = lambda face: jnp.concatenate([face, face], axis=0)
    length = scalars.shape[2]
    flux_x = []
    for x in range(width_x + 1):
        face = doubled(faces_x[x])
        flux_x.append(jnp.where(face > 0, face * scalars[x], face * scalars[x + 1]))
    moved = []
    for x in range(width_x):
        here, face = scalars[x + 1], doubled(faces_y[x])
        flux_y = jnp.where(face > 0, face * here, face * pltpu.roll(here, length - 1, 1))
        moved.append(
            here - (flux_x[x + 1] - flux_x[x]) - (flux_y - pltpu.roll(flux_y, 1, 1))
        )

    width_y = LANES // width_x
    block = lax.broadcasted_iota(jnp.int32, (2 * slab, LANES), 1) // width_y
    for k in range(length // LANES):
        rows = [m[:, k * LANES:(k + 1) * LANES] for m in moved]
        for q in range(width_x):
            tile = rows[q]
            for x in range(width_x):
                if x != q:
                    turned = pltpu.roll(rows[x], ((x - q) % width_x) * width_y, 1)
                    tile = jnp.where(block == x, turned, tile)
            packed[k * width_x + q] = tile
    turns = []
    for o in range(1, n_gy):
        peer = at_y(o)
        turns.append(
            pltpu.make_async_remote_copy(
                src_ref=packed.at[peer], dst_ref=fields.at[me_y],
                send_sem=turn_send.at[o], recv_sem=turn_recv.at[o],
                device_id=(me_x, peer), device_id_type=MESH,
            )
        )
    for copy in turns:
        copy.start()
    fields[me_y] = packed[me_y]

    acc = add(acc, cut, resident - cut)
    for copy in moves:
        copy.wait_recv()
    row_of = lax.broadcasted_iota(jnp.int32, slots.shape[1:], 0)
    table = jnp.zeros(slots.shape[1:], jnp.int32)
    for d in range(len(OFFSETS)):
        table = jnp.where(row_of == d, slots[d], table)
    turned = table.T
    for d in range(len(OFFSETS)):
        limit[resident + d * moving:resident + (d + 1) * moving, :] = jnp.broadcast_to(
            turned[:, d:d + 1], (moving, LANES)
        )
    arrived = len(OFFSETS) * moving
    stage_rows(resident, arrived, all_mass, all_weight, all_cells, limit, hi, lo, lev, col)
    acc = add(acc, resident, arrived)
    total = acc.T
    sums[...] = total[:levels] + total[n_lev * PACK:n_lev * PACK + levels]

    for copy in turns:
        copy.wait_recv()
    for copy in halos + moves + turns:
        copy.wait_send()


def exchange_call(n_gx, n_gy, args, levels, cut):
    vapor, mass, leave = args[0], args[4], args[8]
    slab, width_x, length = vapor.shape
    resident, moving = mass.shape[2], leave.shape[3]
    total = resident + len(OFFSETS) * moving
    f32, i32 = jnp.float32, jnp.int32
    vmem, dma = pltpu.VMEM, pltpu.SemaphoreType.DMA
    record = vmem((total, LANES), f32)
    return pl.pallas_call(
        functools.partial(exchange_kernel, n_gx, n_gy, levels, cut),
        out_shape=[
            jax.ShapeDtypeStruct((n_gy, 2 * slab, LANES), f32),
            jax.ShapeDtypeStruct((total, LANES), f32),
            jax.ShapeDtypeStruct((total, LANES), i32),
            jax.ShapeDtypeStruct((levels, LANES), f32),
        ],
        in_specs=[pl.BlockSpec(memory_space=pltpu.HBM)] * len(args),
        out_specs=[pl.BlockSpec(memory_space=vmem)] * 4,
        scratch_shapes=[
            vmem((width_x + 2, 2 * slab, length), f32),
            vmem((width_x + 1, slab, length), f32),
            vmem((width_x, slab, length), f32),
            record,
            vmem((1, resident), i32),
            vmem((len(OFFSETS), len(OFFSETS), moving), i32),
            vmem((total, LANES), i32),
            record, record, record, record,
            vmem((n_gy, 2 * slab, LANES), f32),
            dma((4 * width_x,)), dma((4,)), dma((5,)), dma((5,)),
            dma((len(OFFSETS), 4)), dma((len(OFFSETS), 4)), dma((n_gy,)), dma((n_gy,)),
        ],
        compiler_params=pltpu.CompilerParams(
            collective_id=0, has_side_effects=True
        ),
        name="exchange",
    )(*args)


def column_of(row):
    n = row.shape[1]
    i = lax.broadcasted_iota(jnp.int32, (n, n), 0)
    j = lax.broadcasted_iota(jnp.int32, (n, n), 1)
    return jnp.sum(jnp.where(i == j, row, 0.0), axis=1, keepdims=True)


def settle_matrix(fall, levels):
    keep = 1.0 / (1.0 + fall)
    logs = jnp.log(fall * keep)
    i = lax.broadcasted_iota(jnp.int32, (levels, levels), 0)
    j = lax.broadcasted_iota(jnp.int32, (levels, levels), 1)
    down = jnp.sum(jnp.where(j <= i, logs, 0.0), axis=1, keepdims=True)
    across = jnp.sum(jnp.where(i <= j, column_of(logs), 0.0), axis=0, keepdims=True)
    spread = jnp.where(j >= i, across - down, 0.0)
    return jnp.where(j >= i, column_of(keep) * jnp.exp(spread), 0.0)


def grow_kernel(
    levels, unroll, width_x, fields, sums, mass, cells, sat, fall, vapor, heat, rain, grown, table
):
    moist, warm = [], []
    low = lax.broadcasted_iota(jnp.int32, (8, LANES), 0) < 4
    for k in range(0, fields.shape[0], 2):
        a, b = fields[k], fields[k + 1]
        moist.append(jnp.where(low, a, pltpu.roll(b, 4, 0)))
        warm.append(jnp.where(low, pltpu.roll(a, 4, 0), b))
    moist = jnp.concatenate(moist, axis=0)
    warm = jnp.concatenate(warm, axis=0)
    excess = moist[:levels] - column_of(sat[...]) * jnp.exp(SAT_SLOPE * warm[:levels])
    growth = jnp.exp(GROW_RATE * excess)
    for k in range(levels):
        table[k] = jnp.broadcast_to(growth[k:k + 1], (8, LANES))

    def tile(t, carry):
        rows = pl.ds(pl.multiple_of(t * 8, 8), 8)
        c = cells[rows, :]
        lev, col = c >> 7, c & (LANES - 1)
        got = jnp.zeros((8, LANES), jnp.float32)
        for k in range(levels):
            near = jnp.take_along_axis(table[k], col, axis=1, mode="promise_in_bounds")
            got = jnp.where(lev == k, near, got)
        grown[rows, :] = mass[rows, :] * got
        return carry

    lax.fori_loop(0, mass.shape[0] // 8, tile, 0, unroll=unroll)

    total = sums[...]
    liquid = total * growth
    condensed = total * (growth - 1.0)
    fallen = jnp.dot(
        settle_matrix(fall[...], levels), liquid,
        precision=lax.Precision.HIGHEST, preferred_element_type=jnp.float32,
    )
    width_y = LANES // width_x
    for x in range(width_x):
        rain[:, x, :] = fallen[:, x * width_y:(x + 1) * width_y]
    vapor[...] = jnp.concatenate([moist[:levels] - condensed, moist[levels:]], axis=0).T
    heat[...] = jnp.concatenate([warm[:levels] + LATENT_HEAT * condensed, warm[levels:]], axis=0).T


def grow_call(fields, sums, mass, cells, sat, fall, levels, width_x, unroll=16):
    f32 = jnp.float32
    total = fields.shape[0] * fields.shape[1] // 2
    return pl.pallas_call(
        functools.partial(grow_kernel, levels, unroll, width_x),
        out_shape=[
            jax.ShapeDtypeStruct((LANES, total), f32),
            jax.ShapeDtypeStruct((LANES, total), f32),
            jax.ShapeDtypeStruct((levels, width_x, LANES // width_x), f32),
            jax.ShapeDtypeStruct(mass.shape, f32),
        ],
        scratch_shapes=[pltpu.VMEM((levels, 8, LANES), f32)],
        name="grow_records",
    )(fields, sums, mass, cells, sat, fall)


def local(n_gx, n_gy, vapor_ratio, potential_temp, flow_x, flow_y, sat_ref, fall_rate, *records):
    levels, width_x = sat_ref.shape[0], vapor_ratio.shape[1]
    args = (vapor_ratio, potential_temp, flow_x, flow_y) + records
    resident = records[0].shape[2]
    cut = resident * 3 // 8
    fields, mass, cells, sums = exchange_call(n_gx, n_gy, args, levels, cut)
    vapor, heat, rain, grown = grow_call(
        fields, sums, mass, cells, sat_ref[None], fall_rate[None], levels, width_x
    )
    unfold = lambda columns: columns.reshape(width_x, LANES // width_x, -1).transpose(2, 0, 1)
    return unfold(vapor), unfold(heat), rain, grown[None, None]


def solution(mesh):
    level_rows = P("gy", "gx", None)
    owned = lambda rank: P("gx", "gy", *([None] * (rank - 2)))
    return jax.shard_map(
        functools.partial(local, mesh.shape["gx"], mesh.shape["gy"]),
        mesh=mesh,
        in_specs=(level_rows,) * 4 + (P(), P()) + tuple(owned(r) for r in (4, 4, 4, 3, 5, 5, 5, 4)),
        out_specs=(P(None, "gx", "gy"),) * 3 + (owned(4),),
        check_vma=False,
    )
```

```python
import functools

import jax
import jax.numpy as jnp
from jax import lax
from jax.experimental import pallas as pl
from jax.experimental.pallas import tpu as pltpu
from jax.sharding import PartitionSpec as P

LANES = 128
PACK = 16
SAT_SLOPE = 0.3
GROW_RATE = 0.5
LATENT_HEAT = 2.5
OFFSETS = ((-1, -1), (-1, 0), (-1, 1), (0, -1), (0, 1), (1, -1), (1, 0), (1, 1))
MESH = pl.DeviceIdType.MESH


def stage_rows(tiles, mass, weight, cells, limit, first, hi, lo, lev, col):
    lane = lax.broadcasted_iota(jnp.int32, (8, LANES), 1)

    def pair(t, carry):
        for half in range(2):
            start = t * 16 + half * 8
            at = pl.ds(pl.multiple_of(start, 8), 8)
            to = pl.ds(pl.multiple_of(first + start, 8), 8)
            m = jnp.where(lane < limit[at, :], mass[at, :], 0.0)
            mass[at, :] = m
            p = m * weight[at, :]
            top = p.astype(jnp.bfloat16).astype(jnp.float32)
            c = cells[at, :]
            hi[to, :] = top
            lo[to, :] = p - top
            lev[to, :] = (c >> 7).astype(jnp.float32)
            col[to, :] = (c & (LANES - 1)).astype(jnp.float32)
        return carry

    lax.fori_loop(tiles[0] // 2, tiles[1] // 2, pair, 0)


def add_rows(acc, groups, first, hi, lo, lev, col, n_lev, group):
    bf16 = jnp.bfloat16
    zero = jnp.zeros((PACK, LANES), bf16)
    one = jnp.ones((PACK, LANES), bf16)
    base = lax.broadcasted_iota(jnp.int32, (PACK, LANES), 0)
    marks = [(base + PACK * g).astype(jnp.float32).astype(bf16) for g in range(LANES // PACK)]

    def step(i, acc):
        left, right = [], []
        for k in range(group):
            j = first + i * group + k

            def spread(ref, j=j):
                return jnp.broadcast_to(ref[pl.ds(j, 1), :], (PACK, LANES)).astype(bf16)

            h, l, v, c = spread(hi), spread(lo), spread(lev), spread(col)
            here = [v == marks[g] for g in range(n_lev)]
            picked = [jnp.where(m, h, zero) for m in here] + [jnp.where(m, l, zero) for m in here]
            right.append(jnp.concatenate(picked, axis=0))
            left.append(jnp.concatenate([jnp.where(c == m, one, zero) for m in marks], axis=0))
        left = jnp.concatenate(left, axis=1)
        right = jnp.concatenate(right, axis=1)
        return acc + lax.dot_general(
            left, right, (((1,), (1,)), ((), ())), preferred_element_type=jnp.float32
        )

    return lax.fori_loop(groups[0], groups[1], step, acc)


def exchange_kernel(
    n_gx, n_gy, levels, cut,
    vapor, warm, flow_x, flow_y, sat, fall, mass, weight, cells, counts,
    leave_mass, leave_weight, leave_cells, leave_counts,
    fields, all_mass, all_cells, sums, sat_rows, inverse,
    pair, scalars, faces_x, faces_y, all_weight, counts_in, slots, limit, out_limit, hi, lo, lev, col, packed,
    out_mass, out_weight, out_cells, out_sums, in_sums,
    leave_sem, load_sem, drop_sem, halo_send, halo_recv, move_send, move_recv, turn_send, turn_recv,
):
    me_x, me_y = lax.axis_index("gx"), lax.axis_index("gy")

    def at_x(step):
        return lax.rem(me_x + (step + n_gx), n_gx)

    def at_y(step):
        return lax.rem(me_y + (step + n_gy), n_gy)

    resident = mass.shape[2]
    ways, moving = leave_mass.shape[2], leave_mass.shape[3]
    arriving = ways * moving
    width_x = vapor.shape[1]
    slab = vapor.shape[0]
    n_lev = -(-levels // PACK)
    empty = jnp.zeros((LANES, 2 * n_lev * PACK), jnp.float32)

    barrier = pltpu.get_barrier_semaphore()
    peers = [(me_x, at_y(o)) for o in range(1, n_gy)]
    peers += [(at_x(dx), at_y(dy)) for dx in (-1, 1) for dy in (-1, 0, 1)]
    for peer in peers:
        pl.semaphore_signal(barrier, inc=1, device_id=peer, device_id_type=MESH)

    leaves = [pltpu.make_async_copy(leave_counts.at[0, 0], slots, leave_sem.at[3, 0])]
    for d in range(ways):
        rows = pl.ds(d * moving, moving)
        leaves += [
            pltpu.make_async_copy(leave_mass.at[0, 0, d], out_mass.at[rows], leave_sem.at[0, d]),
            pltpu.make_async_copy(leave_weight.at[0, 0, d], out_weight.at[rows], leave_sem.at[1, d]),
            pltpu.make_async_copy(leave_cells.at[0, 0, d], out_cells.at[rows], leave_sem.at[2, d]),
        ]
    loads = []
    for x in range(width_x):
        for source, target in (
            (vapor, scalars.at[x + 1, pl.ds(0, slab)]),
            (warm, scalars.at[x + 1, pl.ds(slab, slab)]),
            (flow_x, faces_x.at[x + 1]),
            (flow_y, faces_y.at[x]),
        ):
            loads.append(pltpu.make_async_copy(source.at[:, x, :], target, load_sem.at[len(loads)]))
    for source, k in ((sat, 0), (fall, 1)):
        loads.append(pltpu.make_async_copy(source, pair.at[k], load_sem.at[len(loads)]))
    drops = [
        pltpu.make_async_copy(counts.at[0], counts_in, drop_sem.at[0]),
        pltpu.make_async_copy(mass.at[0, 0], all_mass.at[pl.ds(0, resident)], drop_sem.at[1]),
        pltpu.make_async_copy(weight.at[0, 0], all_weight, drop_sem.at[2]),
        pltpu.make_async_copy(cells.at[0, 0], all_cells.at[pl.ds(0, resident)], drop_sem.at[3]),
    ]
    for copy in leaves + loads + drops:
        copy.start()

    early = jnp.where(me_x < 2, 1, 0)
    group = 16
    add = functools.partial(add_rows, hi=hi, lo=lo, lev=lev, col=col, n_lev=n_lev, group=group)

    def by_level(acc):
        total = acc.T
        return total[:levels] + total[n_lev * PACK:n_lev * PACK + levels]

    def leaving_records(lower, upper):
        stage_rows(
            (lower * (arriving // 8), upper * (arriving // 8)),
            out_mass, out_weight, out_cells, out_limit, resident, hi, lo, lev, col,
        )

        def one_way(d, carry):
            out_sums[d] = by_level(add(empty, (0, moving // group), resident + d * moving))
            return carry

        lax.fori_loop(lower * ways, upper * ways, one_way, 0)

    def resident_rows(lower, upper):
        tiles = (lower * (resident // 8), upper * (resident // 8))
        stage_rows(tiles, all_mass, all_weight, all_cells, limit, 0, hi, lo, lev, col)

    for copy in leaves:
        copy.wait()
    turned = slots[...].T
    for d in range(ways):
        out_limit[d * moving:(d + 1) * moving, :] = jnp.broadcast_to(
            turned[:, d:d + 1], (moving, LANES)
        )
    leaving_records(0, early)
    for copy in drops:
        copy.wait()
    for k in range(resident // LANES):
        row = counts_in[:, k * LANES:(k + 1) * LANES]
        turned = jnp.broadcast_to(row, (8, LANES)).T
        limit[k * LANES:(k + 1) * LANES, :] = jnp.broadcast_to(turned[:, 0:1], (LANES, LANES))
    resident_rows(0, early)
    ahead = early * (cut // group)
    acc = add(empty, (0, ahead), 0)

    for copy in loads:
        copy.wait()
    pl.semaphore_wait(barrier, len(peers))

    halos = []
    for source, step, target in (
        (scalars.at[width_x], 1, scalars.at[0]),
        (faces_x.at[width_x], 1, faces_x.at[0]),
        (scalars.at[1], -1, scalars.at[width_x + 1]),
    ):
        k = len(halos)
        halos.append(
            pltpu.make_async_remote_copy(
                src_ref=source, dst_ref=target,
                send_sem=halo_send.at[k], recv_sem=halo_recv.at[k],
                device_id=(at_x(step), me_y), device_id_type=MESH,
            )
        )
    for copy in halos:
        copy.start()

    leaving_records(early, 1)

    moves = []
    for d, (dx, dy) in enumerate(OFFSETS):
        mine = pl.ds(d * moving, moving)
        theirs = pl.ds(resident + d * moving, moving)
        for k, (source, target) in enumerate((
            (out_mass.at[mine], all_mass.at[theirs]),
            (out_cells.at[mine], all_cells.at[theirs]),
            (out_sums.at[d], in_sums.at[d]),
        )):
            moves.append(
                pltpu.make_async_remote_copy(
                    src_ref=source, dst_ref=target,
                    send_sem=move_send.at[d, k], recv_sem=move_recv.at[d, k],
                    device_id=(at_x(dx), at_y(dy)), device_id_type=MESH,
                )
            )
    for copy in moves:
        copy.start()
    sat_rows[...] = jnp.broadcast_to(column_of(pair[0]), sat_rows.shape)
    inverse[...] = settle_matrix(pair[1], levels)

    for copy in halos:
        copy.wait_recv()
    doubled = lambda face: jnp.concatenate([face, face], axis=0)
    length = scalars.shape[2]
    flux_x = []
    for x in range(width_x + 1):
        face = doubled(faces_x[x])
        flux_x.append(jnp.where(face > 0, face * scalars[x], face * scalars[x + 1]))
    moved = []
    for x in range(width_x):
        here, face = scalars[x + 1], doubled(faces_y[x])
        flux_y = jnp.where(face > 0, face * here, face * pltpu.roll(here, length - 1, 1))
        moved.append(
            here - (flux_x[x + 1] - flux_x[x]) - (flux_y - pltpu.roll(flux_y, 1, 1))
        )

    width_y = LANES // width_x
    block = lax.broadcasted_iota(jnp.int32, (2 * slab, LANES), 1) // width_y
    for k in range(length // LANES):
        rows = [m[:, k * LANES:(k + 1) * LANES] for m in moved]
        for q in range(width_x):
            tile = rows[q]
            for x in range(width_x):
                if x != q:
                    turned = pltpu.roll(rows[x], ((x - q) % width_x) * width_y, 1)
                    tile = jnp.where(block == x, turned, tile)
            packed[k * width_x + q] = tile
    turns = []
    for o in range(1, n_gy):
        peer = at_y(o)
        turns.append(
            pltpu.make_async_remote_copy(
                src_ref=packed.at[peer], dst_ref=fields.at[me_y],
                send_sem=turn_send.at[o], recv_sem=turn_recv.at[o],
                device_id=(me_x, peer), device_id_type=MESH,
            )
        )
    for copy in turns:
        copy.start()
    fields[me_y] = packed[me_y]

    resident_rows(early, 1)
    acc = add(acc, (ahead, resident // group), 0)
    total = by_level(acc)
    for copy in moves:
        copy.wait_recv()
    for d in range(ways):
        total = total + in_sums[d]
    sums[...] = total

    for copy in turns:
        copy.wait_recv()
    for copy in halos + moves + turns:
        copy.wait_send()


def exchange_call(n_gx, n_gy, args, levels, cut):
    vapor, mass, leave = args[0], args[6], args[10]
    slab, width_x, length = vapor.shape
    resident, moving = mass.shape[2], leave.shape[3]
    total = resident + len(OFFSETS) * moving
    f32, i32 = jnp.float32, jnp.int32
    vmem, dma = pltpu.VMEM, pltpu.SemaphoreType.DMA
    record, staged = vmem((resident, LANES), f32), vmem((total, LANES), f32)
    leaving = vmem((total - resident, LANES), f32)
    return pl.pallas_call(
        functools.partial(exchange_kernel, n_gx, n_gy, levels, cut),
        out_shape=[
            vmem((n_gy, 2 * slab, LANES), f32),
            vmem((total, LANES), f32),
            vmem((total, LANES), i32),
            vmem((levels, LANES), f32),
            vmem((levels, LANES), f32),
            vmem((levels, levels), f32),
        ],
        in_specs=[pl.BlockSpec(memory_space=pltpu.HBM)] * len(args),
        out_specs=[pl.BlockSpec(memory_space=vmem)] * 6,
        scratch_shapes=[
            vmem((2, 1, levels), f32),
            vmem((width_x + 2, 2 * slab, length), f32),
            vmem((width_x + 1, slab, length), f32),
            vmem((width_x, slab, length), f32),
            record,
            vmem((1, resident), i32),
            vmem((len(OFFSETS), moving), i32),
            vmem((resident, LANES), i32),
            vmem((total - resident, LANES), i32),
            staged, staged, staged, staged,
            vmem((n_gy, 2 * slab, LANES), f32),
            leaving, leaving, vmem(leaving.shape, i32),
            vmem((len(OFFSETS), levels, LANES), f32),
            vmem((len(OFFSETS), levels, LANES), f32),
            dma((4, len(OFFSETS))),
            dma((4 * width_x + 2,)), dma((4,)), dma((3,)), dma((3,)),
            dma((len(OFFSETS), 3)), dma((len(OFFSETS), 3)), dma((n_gy,)), dma((n_gy,)),
        ],
        compiler_params=pltpu.CompilerParams(
            collective_id=0, has_side_effects=True, vmem_limit_bytes=16 * 1024 * 1024
        ),
        name="exchange",
    )(*(pltpu.with_memory_space_constraint(a, pltpu.HBM) for a in args))


def column_of(row):
    n = row.shape[1]
    i = lax.broadcasted_iota(jnp.int32, (n, n), 0)
    j = lax.broadcasted_iota(jnp.int32, (n, n), 1)
    return jnp.sum(jnp.where(i == j, row, 0.0), axis=1, keepdims=True)


def settle_matrix(fall, levels):
    keep = 1.0 / (1.0 + fall)
    logs = jnp.log(fall * keep)
    i = lax.broadcasted_iota(jnp.int32, (levels, levels), 0)
    j = lax.broadcasted_iota(jnp.int32, (levels, levels), 1)
    down = jnp.sum(jnp.where(j <= i, logs, 0.0), axis=1, keepdims=True)
    across = jnp.sum(jnp.where(i <= j, column_of(logs), 0.0), axis=0, keepdims=True)
    spread = jnp.where(j >= i, across - down, 0.0)
    return jnp.where(j >= i, column_of(keep) * jnp.exp(spread), 0.0)


def grow_kernel(
    levels, chunks, width_x,
    fields, sums, sat_rows, inverse, mass, cells,
    vapor_out, heat_out, rain_out, grown_out,
    table, vapor, heat, rain, grown, sem,
):
    moist, warm = [], []
    low = lax.broadcasted_iota(jnp.int32, (8, LANES), 0) < 4
    for k in range(0, fields.shape[0], 2):
        a, b = fields[k], fields[k + 1]
        moist.append(jnp.where(low, a, pltpu.roll(b, 4, 0)))
        warm.append(jnp.where(low, pltpu.roll(a, 4, 0), b))
    moist = jnp.concatenate(moist, axis=0)
    warm = jnp.concatenate(warm, axis=0)
    excess = moist[:levels] - sat_rows[...] * jnp.exp(SAT_SLOPE * warm[:levels])
    growth = jnp.exp(GROW_RATE * excess)
    for k in range(levels):
        table[k] = jnp.broadcast_to(growth[k:k + 1], (8, LANES))

    total = sums[...]
    condensed = total * (growth - 1.0)
    vapor[...] = jnp.concatenate([moist[:levels] - condensed, moist[levels:]], axis=0).T
    heat[...] = jnp.concatenate([warm[:levels] + LATENT_HEAT * condensed, warm[levels:]], axis=0).T
    fallen = jnp.dot(
        inverse[...], total * growth,
        precision=lax.Precision.HIGHEST, preferred_element_type=jnp.float32,
    )
    width_y = LANES // width_x
    for x in range(width_x):
        rain[:, x, :] = fallen[:, x * width_y:(x + 1) * width_y]
    copies = [
        pltpu.make_async_copy(vapor, vapor_out, sem.at[0]),
        pltpu.make_async_copy(heat, heat_out, sem.at[1]),
        pltpu.make_async_copy(rain, rain_out, sem.at[2]),
    ]
    for copy in copies:
        copy.start()

    size = mass.shape[0] // chunks

    def tile(start, t):
        rows = pl.ds(pl.multiple_of(start + t * 8, 8), 8)
        c = cells[rows, :]
        lev, col = c >> 7, c & (LANES - 1)
        got = jnp.zeros((8, LANES), jnp.float32)
        for k in range(levels):
            near = jnp.take_along_axis(table[k], col, axis=1, mode="promise_in_bounds")
            got = jnp.where(lev == k, near, got)
        grown[rows, :] = mass[rows, :] * got

    def chunk(i, carry):
        start = pl.multiple_of(i * size, 8)
        for t in range(size // 8):
            tile(start, t)
        part = pl.ds(start, size)
        pltpu.make_async_copy(grown.at[part], grown_out.at[part], sem.at[3 + i]).start()
        return carry

    lax.fori_loop(0, chunks, chunk, 0)
    for i in range(chunks):
        part = pl.ds(i * size, size)
        copies.append(pltpu.make_async_copy(grown.at[part], grown_out.at[part], sem.at[3 + i]))
    for copy in copies:
        copy.wait()


def grow_call(fields, mass, cells, sums, sat_rows, inverse, width_x, chunks=4):
    f32 = jnp.float32
    levels, total = sums.shape[0], fields.shape[0] * fields.shape[1] // 2
    shapes = [(LANES, total), (LANES, total), (levels, width_x, LANES // width_x), mass.shape]
    return pl.pallas_call(
        functools.partial(grow_kernel, levels, chunks, width_x),
        out_shape=[jax.ShapeDtypeStruct(s, f32) for s in shapes],
        in_specs=[pl.BlockSpec(memory_space=pltpu.VMEM)] * 6,
        out_specs=[pl.BlockSpec(memory_space=pltpu.HBM)] * 4,
        scratch_shapes=[pltpu.VMEM((levels, 8, LANES), f32)]
        + [pltpu.VMEM(s, f32) for s in shapes]
        + [pltpu.SemaphoreType.DMA((3 + chunks,))],
        compiler_params=pltpu.CompilerParams(vmem_limit_bytes=16 * 1024 * 1024),
        name="grow_records",
    )(fields, sums, sat_rows, inverse, mass, cells)


def local(n_gx, n_gy, vapor_ratio, potential_temp, flow_x, flow_y, sat_ref, fall_rate, *records):
    levels, width_x = sat_ref.shape[0], vapor_ratio.shape[1]
    args = (vapor_ratio, potential_temp, flow_x, flow_y, sat_ref[None], fall_rate[None]) + records
    resident = records[0].shape[2]
    cut = resident * 5 // 8
    handed = exchange_call(n_gx, n_gy, args, levels, cut)
    vapor, heat, rain, grown = grow_call(*handed, width_x)
    unfold = lambda columns: columns.reshape(width_x, LANES // width_x, -1).transpose(2, 0, 1)
    return unfold(vapor), unfold(heat), rain, grown[None, None]


def solution(mesh):
    level_rows = P("gy", "gx", None)
    owned = lambda rank: P("gx", "gy", *([None] * (rank - 2)))
    return jax.shard_map(
        functools.partial(local, mesh.shape["gx"], mesh.shape["gy"]),
        mesh=mesh,
        in_specs=(level_rows,) * 4 + (P(), P()) + tuple(owned(r) for r in (4, 4, 4, 3, 5, 5, 5, 4)),
        out_specs=(P(None, "gx", "gy"),) * 3 + (owned(4),),
        check_vma=False,
    )
```

```python
import functools

import jax
import jax.numpy as jnp
from jax import lax
from jax.experimental import pallas as pl
from jax.experimental.pallas import tpu as pltpu
from jax.sharding import PartitionSpec as P

LANES = 128
PACK = 16
SAT_SLOPE = 0.3
GROW_RATE = 0.5
LATENT_HEAT = 2.5
OFFSETS = ((-1, -1), (-1, 0), (-1, 1), (0, -1), (0, 1), (1, -1), (1, 0), (1, 1))
MESH = pl.DeviceIdType.MESH


def stage_rows(blocks, mass, weight, cells, limit, first, hi, lo, lev, col):
    lane = lax.broadcasted_iota(jnp.int32, (8, LANES), 1)

    def block(t, carry):
        for half in range(2):
            at = pl.ds(half * 8, 8)
            to = pl.ds(pl.multiple_of(first + t * 16 + half * 8, 8), 8)
            m = jnp.where(lane < limit[to, :], mass[t, at, :], 0.0)
            mass[t, at, :] = m
            p = m * weight[t, at, :]
            top = p.astype(jnp.bfloat16).astype(jnp.float32)
            c = cells[t, at, :]
            hi[to, :] = top
            lo[to, :] = p - top
            lev[to, :] = (c >> 7).astype(jnp.float32)
            col[to, :] = (c & (LANES - 1)).astype(jnp.float32)
        return carry

    lax.fori_loop(blocks[0], blocks[1], block, 0)


def add_rows(acc, groups, first, hi, lo, lev, col, n_lev, group):
    bf16 = jnp.bfloat16
    zero = jnp.zeros((PACK, LANES), bf16)
    one = jnp.ones((PACK, LANES), bf16)
    base = lax.broadcasted_iota(jnp.int32, (PACK, LANES), 0)
    marks = [(base + PACK * g).astype(jnp.float32).astype(bf16) for g in range(LANES // PACK)]

    def step(i, acc):
        left, right = [], []
        for k in range(group):
            j = first + i * group + k

            def spread(ref, j=j):
                return jnp.broadcast_to(ref[pl.ds(j, 1), :], (PACK, LANES)).astype(bf16)

            h, l, v, c = spread(hi), spread(lo), spread(lev), spread(col)
            here = [v == marks[g] for g in range(n_lev)]
            picked = [jnp.where(m, h, zero) for m in here] + [jnp.where(m, l, zero) for m in here]
            right.append(jnp.concatenate(picked, axis=0))
            left.append(jnp.concatenate([jnp.where(c == m, one, zero) for m in marks], axis=0))
        left = jnp.concatenate(left, axis=1)
        right = jnp.concatenate(right, axis=1)
        return acc + lax.dot_general(
            left, right, (((1,), (1,)), ((), ())), preferred_element_type=jnp.float32
        )

    return lax.fori_loop(groups[0], groups[1], step, acc)


def exchange_kernel(
    n_gx, n_gy, levels, cut,
    vapor, warm, flow_x, flow_y, sat, fall, mass, weight, cells, counts,
    leave_mass, leave_weight, leave_cells, leave_counts,
    fields, all_mass, all_cells, sums, sat_rows, inverse,
    pair, scalars, faces_x, faces_y, all_weight, counts_in, slots, limit, hi, lo, lev, col, packed,
    out_mass, out_weight, out_cells, out_sums, in_sums,
    own_sem, halo_send, halo_recv, move_send, move_recv, turn_sem,
):
    me_x, me_y = lax.axis_index("gx"), lax.axis_index("gy")

    def at_x(step):
        return lax.rem(me_x + (step + n_gx), n_gx)

    def at_y(step):
        return lax.rem(me_y + (step + n_gy), n_gy)

    resident = mass.shape[2] * mass.shape[3]
    own_mass, own_cells = all_mass.at[pl.ds(0, mass.shape[2])], all_cells.at[pl.ds(0, mass.shape[2])]
    ways, moving = leave_mass.shape[2], leave_mass.shape[3]
    arriving = ways * moving
    width_x = vapor.shape[1]
    slab = vapor.shape[0]
    n_lev = -(-levels // PACK)
    empty = jnp.zeros((LANES, 2 * n_lev * PACK), jnp.float32)

    barrier = pltpu.get_barrier_semaphore()
    peers = [(me_x, at_y(o)) for o in range(1, n_gy)]
    peers += [(at_x(dx), at_y(dy)) for dx in (-1, 1) for dy in (-1, 0, 1)]
    for peer in peers:
        pl.semaphore_signal(barrier, inc=1, device_id=peer, device_id_type=MESH)

    leaves = [
        pltpu.make_async_copy(leave_counts.at[0, 0], slots, own_sem.at[0]),
        pltpu.make_async_copy(leave_mass.at[0, 0], out_mass, own_sem.at[1]),
        pltpu.make_async_copy(leave_weight.at[0, 0], out_weight, own_sem.at[2]),
        pltpu.make_async_copy(leave_cells.at[0, 0], out_cells, own_sem.at[3]),
    ]
    loads = []
    for x in range(width_x):
        loads += [
            pltpu.make_async_copy(vapor.at[:, x, :], scalars.at[x + 1, pl.ds(0, slab)], own_sem.at[4]),
            pltpu.make_async_copy(warm.at[:, x, :], scalars.at[x + 1, pl.ds(slab, slab)], own_sem.at[4]),
            pltpu.make_async_copy(flow_x.at[:, x, :], faces_x.at[x + 1], own_sem.at[5]),
            pltpu.make_async_copy(flow_y.at[:, x, :], faces_y.at[x], own_sem.at[6]),
        ]
    loads += [
        pltpu.make_async_copy(sat, pair.at[0], own_sem.at[7]),
        pltpu.make_async_copy(fall, pair.at[1], own_sem.at[7]),
    ]
    drops = [
        pltpu.make_async_copy(counts.at[0], counts_in, own_sem.at[8]),
        pltpu.make_async_copy(mass.at[0, 0], own_mass, own_sem.at[9]),
        pltpu.make_async_copy(weight.at[0, 0], all_weight, own_sem.at[10]),
        pltpu.make_async_copy(cells.at[0, 0], own_cells, own_sem.at[11]),
    ]

    def all_of(ref, sem):
        return pltpu.make_async_copy(ref, ref, sem)

    for copy in leaves + loads + drops:
        copy.start()

    early = jnp.where(me_x < 2, 1, 0)
    group = 16
    add = functools.partial(add_rows, hi=hi, lo=lo, lev=lev, col=col, n_lev=n_lev, group=group)

    def by_level(acc):
        total = acc.T
        return total[:levels] + total[n_lev * PACK:n_lev * PACK + levels]

    def leaving_records(lower, upper):
        stage_rows(
            (lower * ways, upper * ways),
            out_mass, out_weight, out_cells, limit, resident, hi, lo, lev, col,
        )

        def one_way(d, carry):
            out_sums[d] = by_level(add(empty, (0, moving // group), resident + d * moving))
            return carry

        lax.fori_loop(lower * ways, upper * ways, one_way, 0)

    def resident_rows(lower, upper):
        blocks = (lower * (resident // 16), upper * (resident // 16))
        stage_rows(blocks, all_mass, all_weight, all_cells, limit, 0, hi, lo, lev, col)

    for copy in leaves:
        copy.wait()
    turned = slots[...].T
    for d in range(ways):
        limit[resident + d * moving:resident + (d + 1) * moving, :] = jnp.broadcast_to(
            turned[:, d:d + 1], (moving, LANES)
        )
    leaving_records(0, early)
    for copy in drops:
        copy.wait()
    for k in range(resident // LANES):
        row = counts_in[:, k * LANES:(k + 1) * LANES]
        turned = jnp.broadcast_to(row, (8, LANES)).T
        limit[k * LANES:(k + 1) * LANES, :] = jnp.broadcast_to(turned[:, 0:1], (LANES, LANES))
    resident_rows(0, early)
    ahead = early * (cut // group)
    acc = add(empty, (0, ahead), 0)

    all_of(scalars.at[pl.ds(1, width_x)], own_sem.at[4]).wait()
    all_of(faces_x.at[pl.ds(1, width_x)], own_sem.at[5]).wait()
    all_of(faces_y, own_sem.at[6]).wait()
    all_of(pair, own_sem.at[7]).wait()
    pl.semaphore_wait(barrier, len(peers))

    halos = []
    for source, step, target in (
        (scalars.at[width_x], 1, scalars.at[0]),
        (faces_x.at[width_x], 1, faces_x.at[0]),
        (scalars.at[1], -1, scalars.at[width_x + 1]),
    ):
        k = len(halos)
        halos.append(
            pltpu.make_async_remote_copy(
                src_ref=source, dst_ref=target,
                send_sem=halo_send.at[k], recv_sem=halo_recv.at[k],
                device_id=(at_x(step), me_y), device_id_type=MESH,
            )
        )
    for copy in halos:
        copy.start()

    leaving_records(early, 1)

    moves = []
    for d, (dx, dy) in enumerate(OFFSETS):
        for k, (source, target) in enumerate((
            (out_mass.at[d], all_mass.at[mass.shape[2] + d]),
            (out_cells.at[d], all_cells.at[mass.shape[2] + d]),
            (out_sums.at[d], in_sums.at[d]),
        )):
            moves.append(
                pltpu.make_async_remote_copy(
                    src_ref=source, dst_ref=target,
                    send_sem=move_send.at[k], recv_sem=move_recv.at[k],
                    device_id=(at_x(dx), at_y(dy)), device_id_type=MESH,
                )
            )
    for copy in moves:
        copy.start()
    sat_rows[...] = jnp.broadcast_to(column_of(pair[0]), sat_rows.shape)
    inverse[...] = settle_matrix(pair[1], levels)

    for copy in halos:
        copy.wait_recv()
    doubled = lambda face: jnp.concatenate([face, face], axis=0)
    length = scalars.shape[2]
    flux_x = []
    for x in range(width_x + 1):
        face = doubled(faces_x[x])
        flux_x.append(jnp.where(face > 0, face * scalars[x], face * scalars[x + 1]))
    moved = []
    for x in range(width_x):
        here, face = scalars[x + 1], doubled(faces_y[x])
        flux_y = jnp.where(face > 0, face * here, face * pltpu.roll(here, length - 1, 1))
        moved.append(
            here - (flux_x[x + 1] - flux_x[x]) - (flux_y - pltpu.roll(flux_y, 1, 1))
        )

    width_y = LANES // width_x
    block = lax.broadcasted_iota(jnp.int32, (2 * slab, LANES), 1) // width_y
    for k in range(length // LANES):
        rows = [m[:, k * LANES:(k + 1) * LANES] for m in moved]
        for q in range(width_x):
            tile = rows[q]
            for x in range(width_x):
                if x != q:
                    turned = pltpu.roll(rows[x], ((x - q) % width_x) * width_y, 1)
                    tile = jnp.where(block == x, turned, tile)
            packed[k * width_x + q] = tile
    turns = []
    for o in range(1, n_gy):
        peer = at_y(o)
        turns.append(
            pltpu.make_async_remote_copy(
                src_ref=packed.at[peer], dst_ref=fields.at[me_y],
                send_sem=turn_sem.at[0], recv_sem=turn_sem.at[1],
                device_id=(me_x, peer), device_id_type=MESH,
            )
        )
    for copy in turns:
        copy.start()
    fields[me_y] = packed[me_y]

    resident_rows(early, 1)
    acc = add(acc, (ahead, resident // group), 0)
    total = by_level(acc)
    for k, ref in enumerate((out_mass, out_cells, in_sums)):
        all_of(ref, move_recv.at[k]).wait()
    for d in range(ways):
        total = total + in_sums[d]
    sums[...] = total

    others = packed.at[pl.ds(0, n_gy - 1)]
    all_of(others, turn_sem.at[1]).wait()
    for copy in halos:
        copy.wait_send()
    for k, ref in enumerate((out_mass, out_cells, out_sums)):
        all_of(ref, move_send.at[k]).wait()
    all_of(others, turn_sem.at[0]).wait()


def exchange_call(n_gx, n_gy, args, levels, cut):
    vapor, mass, leave = args[0], args[6], args[10]
    slab, width_x, length = vapor.shape
    resident, moving = mass.shape[2] * mass.shape[3], leave.shape[3]
    total = resident + len(OFFSETS) * moving
    f32, i32 = jnp.float32, jnp.int32
    vmem, dma = pltpu.VMEM, pltpu.SemaphoreType.DMA
    record, staged = vmem(mass.shape[2:], f32), vmem((total, LANES), f32)
    leaving = vmem(leave.shape[2:], f32)
    return pl.pallas_call(
        functools.partial(exchange_kernel, n_gx, n_gy, levels, cut),
        out_shape=[
            vmem((n_gy, 2 * slab, LANES), f32),
            vmem((total // moving, moving, LANES), f32),
            vmem((total // moving, moving, LANES), i32),
            vmem((levels, LANES), f32),
            vmem((levels, LANES), f32),
            vmem((levels, levels), f32),
        ],
        in_specs=[pl.BlockSpec(memory_space=pltpu.HBM)] * len(args),
        out_specs=[pl.BlockSpec(memory_space=vmem)] * 6,
        scratch_shapes=[
            vmem((2, 1, levels), f32),
            vmem((width_x + 2, 2 * slab, length), f32),
            vmem((width_x + 1, slab, length), f32),
            vmem((width_x, slab, length), f32),
            record,
            vmem((1, resident), i32),
            vmem((len(OFFSETS), moving), i32),
            vmem((total, LANES), i32),
            staged, staged, staged, staged,
            vmem((n_gy, 2 * slab, LANES), f32),
            leaving, leaving, vmem(leaving.shape, i32),
            vmem((len(OFFSETS), levels, LANES), f32),
            vmem((len(OFFSETS), levels, LANES), f32),
            dma((12,)), dma((3,)), dma((3,)), dma((3,)), dma((3,)), dma((2,)),
        ],
        compiler_params=pltpu.CompilerParams(
            collective_id=0, has_side_effects=True, vmem_limit_bytes=16 * 1024 * 1024
        ),
        name="exchange",
    )(*(pltpu.with_memory_space_constraint(a, pltpu.HBM) for a in args))


def column_of(row):
    n = row.shape[1]
    i = lax.broadcasted_iota(jnp.int32, (n, n), 0)
    j = lax.broadcasted_iota(jnp.int32, (n, n), 1)
    return jnp.sum(jnp.where(i == j, row, 0.0), axis=1, keepdims=True)


def settle_matrix(fall, levels):
    keep = 1.0 / (1.0 + fall)
    logs = jnp.log(fall * keep)
    i = lax.broadcasted_iota(jnp.int32, (levels, levels), 0)
    j = lax.broadcasted_iota(jnp.int32, (levels, levels), 1)
    down = jnp.sum(jnp.where(j <= i, logs, 0.0), axis=1, keepdims=True)
    across = jnp.sum(jnp.where(i <= j, column_of(logs), 0.0), axis=0, keepdims=True)
    spread = jnp.where(j >= i, across - down, 0.0)
    return jnp.where(j >= i, column_of(keep) * jnp.exp(spread), 0.0)


def grow_kernel(
    levels, chunks, width_x,
    fields, sums, sat_rows, inverse, mass, cells,
    vapor_out, heat_out, rain_out, grown_out,
    table, vapor, heat, rain, grown, sem,
):
    moist, warm = [], []
    low = lax.broadcasted_iota(jnp.int32, (8, LANES), 0) < 4
    for k in range(0, fields.shape[0], 2):
        a, b = fields[k], fields[k + 1]
        moist.append(jnp.where(low, a, pltpu.roll(b, 4, 0)))
        warm.append(jnp.where(low, pltpu.roll(a, 4, 0), b))
    moist = jnp.concatenate(moist, axis=0)
    warm = jnp.concatenate(warm, axis=0)
    excess = moist[:levels] - sat_rows[...] * jnp.exp(SAT_SLOPE * warm[:levels])
    growth = jnp.exp(GROW_RATE * excess)
    for k in range(levels):
        table[k] = jnp.broadcast_to(growth[k:k + 1], (8, LANES))

    total = sums[...]
    condensed = total * (growth - 1.0)
    vapor[...] = jnp.concatenate([moist[:levels] - condensed, moist[levels:]], axis=0).T
    heat[...] = jnp.concatenate([warm[:levels] + LATENT_HEAT * condensed, warm[levels:]], axis=0).T
    fallen = jnp.dot(
        inverse[...], total * growth,
        precision=lax.Precision.HIGHEST, preferred_element_type=jnp.float32,
    )
    width_y = LANES // width_x
    for x in range(width_x):
        rain[:, x, :] = fallen[:, x * width_y:(x + 1) * width_y]
    copies = [
        pltpu.make_async_copy(vapor, vapor_out, sem.at[0]),
        pltpu.make_async_copy(heat, heat_out, sem.at[1]),
        pltpu.make_async_copy(rain, rain_out, sem.at[2]),
    ]
    for copy in copies:
        copy.start()

    size = mass.shape[0] // chunks

    def tile(start, t):
        rows = pl.ds(pl.multiple_of(start + t * 8, 8), 8)
        c = cells[rows, :]
        lev, col = c >> 7, c & (LANES - 1)
        got = jnp.zeros((8, LANES), jnp.float32)
        for k in range(levels):
            near = jnp.take_along_axis(table[k], col, axis=1, mode="promise_in_bounds")
            got = jnp.where(lev == k, near, got)
        grown[rows, :] = mass[rows, :] * got

    def chunk(i, carry):
        start = pl.multiple_of(i * size, 8)
        for t in range(size // 8):
            tile(start, t)
        part = pl.ds(start, size)
        pltpu.make_async_copy(grown.at[part], grown_out.at[part], sem.at[3 + i]).start()
        return carry

    lax.fori_loop(0, chunks, chunk, 0)
    for i in range(chunks):
        part = pl.ds(i * size, size)
        copies.append(pltpu.make_async_copy(grown.at[part], grown_out.at[part], sem.at[3 + i]))
    for copy in copies:
        copy.wait()


def grow_call(fields, mass, cells, sums, sat_rows, inverse, width_x, chunks=4):
    f32 = jnp.float32
    levels, total = sums.shape[0], fields.shape[0] * fields.shape[1] // 2
    shapes = [(LANES, total), (LANES, total), (levels, width_x, LANES // width_x), mass.shape]
    return pl.pallas_call(
        functools.partial(grow_kernel, levels, chunks, width_x),
        out_shape=[jax.ShapeDtypeStruct(s, f32) for s in shapes],
        in_specs=[pl.BlockSpec(memory_space=pltpu.VMEM)] * 6,
        out_specs=[pl.BlockSpec(memory_space=pltpu.HBM)] * 4,
        scratch_shapes=[pltpu.VMEM((levels, 8, LANES), f32)]
        + [pltpu.VMEM(s, f32) for s in shapes]
        + [pltpu.SemaphoreType.DMA((3 + chunks,))],
        compiler_params=pltpu.CompilerParams(vmem_limit_bytes=16 * 1024 * 1024),
        name="grow_records",
    )(fields, sums, sat_rows, inverse, mass, cells)


def local(n_gx, n_gy, vapor_ratio, potential_temp, flow_x, flow_y, sat_ref, fall_rate, *records):
    levels, width_x = sat_ref.shape[0], vapor_ratio.shape[1]
    args = (vapor_ratio, potential_temp, flow_x, flow_y, sat_ref[None], fall_rate[None]) + records
    resident = records[0].shape[2]
    cut = resident * 5 // 8
    moving = records[4].shape[3]
    blocks = lambda a: a.reshape(1, 1, resident // moving, moving, LANES)
    args = args[:6] + tuple(blocks(a) for a in args[6:9]) + args[9:]
    handed = list(exchange_call(n_gx, n_gy, args, levels, cut))
    handed[1], handed[2] = (h.reshape(-1, LANES) for h in handed[1:3])
    vapor, heat, rain, grown = grow_call(*handed, width_x)
    unfold = lambda columns: columns.reshape(width_x, LANES // width_x, -1).transpose(2, 0, 1)
    return unfold(vapor), unfold(heat), rain, grown[None, None]


def solution(mesh):
    level_rows = P("gy", "gx", None)
    owned = lambda rank: P("gx", "gy", *([None] * (rank - 2)))
    return jax.shard_map(
        functools.partial(local, mesh.shape["gx"], mesh.shape["gy"]),
        mesh=mesh,
        in_specs=(level_rows,) * 4 + (P(), P()) + tuple(owned(r) for r in (4, 4, 4, 3, 5, 5, 5, 4)),
        out_specs=(P(None, "gx", "gy"),) * 3 + (owned(4),),
        check_vma=False,
    )
```

```python
import functools

import jax
import jax.numpy as jnp
from jax import lax
from jax.experimental import pallas as pl
from jax.experimental.pallas import tpu as pltpu
from jax.sharding import PartitionSpec as P

LANES = 128
PACK = 16
SAT_SLOPE = 0.3
GROW_RATE = 0.5
LATENT_HEAT = 2.5
OFFSETS = ((-1, -1), (-1, 0), (-1, 1), (0, -1), (0, 1), (1, -1), (1, 0), (1, 1))
MESH = pl.DeviceIdType.MESH


def stage_rows(blocks, mass, weight, cells, limit, first, hi, lo, lev, col):
    lane = lax.broadcasted_iota(jnp.int32, (8, LANES), 1)

    def block(t, carry):
        for half in range(2):
            at = pl.ds(half * 8, 8)
            to = pl.ds(pl.multiple_of(first + t * 16 + half * 8, 8), 8)
            m = jnp.where(lane < limit[to, :], mass[t, at, :], 0.0)
            mass[t, at, :] = m
            p = m * weight[t, at, :]
            top = p.astype(jnp.bfloat16).astype(jnp.float32)
            c = cells[t, at, :]
            hi[to, :] = top
            lo[to, :] = p - top
            lev[to, :] = (c >> 7).astype(jnp.float32)
            col[to, :] = (c & (LANES - 1)).astype(jnp.float32)
        return carry

    lax.fori_loop(blocks[0], blocks[1], block, 0)


def add_rows(acc, groups, first, hi, lo, lev, col, n_lev, group):
    bf16 = jnp.bfloat16
    zero = jnp.zeros((PACK, LANES), bf16)
    one = jnp.ones((PACK, LANES), bf16)
    base = lax.broadcasted_iota(jnp.int32, (PACK, LANES), 0)
    marks = [(base + PACK * g).astype(jnp.float32).astype(bf16) for g in range(LANES // PACK)]

    def step(i, acc):
        left, right = [], []
        for k in range(group):
            j = first + i * group + k

            def spread(ref, j=j):
                return jnp.broadcast_to(ref[pl.ds(j, 1), :], (PACK, LANES)).astype(bf16)

            h, l, v, c = spread(hi), spread(lo), spread(lev), spread(col)
            here = [v == marks[g] for g in range(n_lev)]
            picked = [jnp.where(m, h, zero) for m in here] + [jnp.where(m, l, zero) for m in here]
            right.append(jnp.concatenate(picked, axis=0))
            left.append(jnp.concatenate([jnp.where(c == m, one, zero) for m in marks], axis=0))
        left = jnp.concatenate(left, axis=1)
        right = jnp.concatenate(right, axis=1)
        return acc + lax.dot_general(
            left, right, (((1,), (1,)), ((), ())), preferred_element_type=jnp.float32
        )

    return lax.fori_loop(groups[0], groups[1], step, acc)


def exchange_kernel(
    n_gx, n_gy, levels, cut,
    vapor, warm, flow_x, flow_y, sat, fall, mass, weight, cells, counts,
    leave_mass, leave_weight, leave_cells, leave_counts,
    fields, all_mass, all_cells, sums, sat_rows, inverse,
    pair, scalars, faces_x, faces_y, all_weight, counts_in, slots, limit, hi, lo, lev, col, packed, edges,
    out_mass, out_weight, out_cells, out_sums, in_sums,
    own_sem, halo_send, halo_recv, move_send, move_recv, turn_sem,
):
    me_x, me_y = lax.axis_index("gx"), lax.axis_index("gy")

    def at_x(step):
        return lax.rem(me_x + (step + n_gx), n_gx)

    def at_y(step):
        return lax.rem(me_y + (step + n_gy), n_gy)

    resident = mass.shape[2] * mass.shape[3]
    own_mass, own_cells = all_mass.at[pl.ds(0, mass.shape[2])], all_cells.at[pl.ds(0, mass.shape[2])]
    ways, moving = leave_mass.shape[2], leave_mass.shape[3]
    arriving = ways * moving
    width_x = vapor.shape[1]
    slab = vapor.shape[0]
    n_lev = -(-levels // PACK)
    empty = jnp.zeros((LANES, 2 * n_lev * PACK), jnp.float32)

    barrier = pltpu.get_barrier_semaphore()
    peers = [(me_x, at_y(o)) for o in range(1, n_gy)]
    peers += [(at_x(dx), at_y(dy)) for dx in (-1, 1) for dy in (-1, 0, 1)]
    for peer in peers:
        pl.semaphore_signal(barrier, inc=1, device_id=peer, device_id_type=MESH)

    leaves = [
        pltpu.make_async_copy(leave_counts.at[0, 0], slots, own_sem.at[0]),
        pltpu.make_async_copy(leave_mass.at[0, 0], out_mass, own_sem.at[1]),
        pltpu.make_async_copy(leave_weight.at[0, 0], out_weight, own_sem.at[2]),
        pltpu.make_async_copy(leave_cells.at[0, 0], out_cells, own_sem.at[3]),
    ]
    loads = []
    for x in range(width_x):
        loads += [
            pltpu.make_async_copy(vapor.at[:, x, :], scalars.at[x + 1, pl.ds(0, slab)], own_sem.at[4]),
            pltpu.make_async_copy(warm.at[:, x, :], scalars.at[x + 1, pl.ds(slab, slab)], own_sem.at[4]),
            pltpu.make_async_copy(flow_x.at[:, x, :], faces_x.at[x + 1], own_sem.at[5]),
            pltpu.make_async_copy(flow_y.at[:, x, :], faces_y.at[x], own_sem.at[6]),
        ]
    loads += [
        pltpu.make_async_copy(sat, pair.at[0], own_sem.at[7]),
        pltpu.make_async_copy(fall, pair.at[1], own_sem.at[7]),
    ]
    drops = [
        pltpu.make_async_copy(counts.at[0], counts_in, own_sem.at[8]),
        pltpu.make_async_copy(mass.at[0, 0], own_mass, own_sem.at[9]),
        pltpu.make_async_copy(weight.at[0, 0], all_weight, own_sem.at[10]),
        pltpu.make_async_copy(cells.at[0, 0], own_cells, own_sem.at[11]),
    ]

    def all_of(ref, sem):
        return pltpu.make_async_copy(ref, ref, sem)

    for copy in leaves + loads + drops:
        copy.start()

    side = 4
    away = lambda v: jnp.minimum(v, side - v)
    hops = away(lax.rem(me_y, side)) + away(me_y // side)
    spare = jnp.where(me_x < 2, 14, 0) + 4 * (side - hops)
    spare += jnp.where((me_x > 1) & (me_x < n_gx - 1), 7 * lax.rem(me_x, 2), 0)
    spare = jnp.where((me_x == 2) | (me_x == n_gx - 1), 0, spare)
    early = jnp.where(spare >= 14, 1, 0)
    ahead = early * jnp.clip(spare - 14, 0, 12)
    group = 16
    add = functools.partial(add_rows, hi=hi, lo=lo, lev=lev, col=col, n_lev=n_lev, group=group)

    def by_level(acc):
        total = acc.T
        return total[:levels] + total[n_lev * PACK:n_lev * PACK + levels]

    def way_sums(d):
        out_sums[d] = by_level(add(empty, (0, moving // group), resident + d * moving))

    def way_copy(d):
        cell = d + d // 4 - d // 8
        return pltpu.make_async_remote_copy(
            src_ref=out_sums.at[d], dst_ref=in_sums.at[d],
            send_sem=move_send.at[2], recv_sem=move_recv.at[2],
            device_id=(at_x(cell // 3 - 1), at_y(cell % 3 - 1)), device_id_type=MESH,
        )

    def resident_rows(lower, upper):
        blocks = (lower * (resident // 16), upper * (resident // 16))
        stage_rows(blocks, all_mass, all_weight, all_cells, limit, 0, hi, lo, lev, col)

    for copy in leaves:
        copy.wait()
    turned = slots[...].T
    for d in range(ways):
        limit[resident + d * moving:resident + (d + 1) * moving, :] = jnp.broadcast_to(
            turned[:, d:d + 1], (moving, LANES)
        )
    stage_rows((0, ways), out_mass, out_weight, out_cells, limit, resident, hi, lo, lev, col)

    def sums_ahead(d, carry):
        way_sums(d)
        return carry

    lax.fori_loop(0, early * ways, sums_ahead, 0)
    for copy in drops:
        copy.wait()
    for k in range(resident // LANES):
        row = counts_in[:, k * LANES:(k + 1) * LANES]
        turned = jnp.broadcast_to(row, (8, LANES)).T
        limit[k * LANES:(k + 1) * LANES, :] = jnp.broadcast_to(turned[:, 0:1], (LANES, LANES))
    resident_rows(0, early)
    acc = add(empty, (0, ahead), 0)

    all_of(scalars.at[pl.ds(1, width_x)], own_sem.at[4]).wait()
    all_of(faces_x.at[pl.ds(1, width_x)], own_sem.at[5]).wait()
    all_of(faces_y, own_sem.at[6]).wait()
    all_of(pair, own_sem.at[7]).wait()
    pl.semaphore_wait(barrier, len(peers))

    halos = []
    for source, step, target in (
        (scalars.at[width_x], 1, scalars.at[0]),
        (faces_x.at[width_x], 1, faces_x.at[0]),
        (scalars.at[1], -1, scalars.at[width_x + 1]),
    ):
        k = len(halos)
        halos.append(
            pltpu.make_async_remote_copy(
                src_ref=source, dst_ref=target,
                send_sem=halo_send.at[k], recv_sem=halo_recv.at[k],
                device_id=(at_x(step), me_y), device_id_type=MESH,
            )
        )
    for copy in halos:
        copy.start()

    moves = []
    for d, (dx, dy) in enumerate(OFFSETS):
        for k, (source, target) in enumerate((
            (out_mass.at[d], all_mass.at[mass.shape[2] + d]),
            (out_cells.at[d], all_cells.at[mass.shape[2] + d]),
        )):
            moves.append(
                pltpu.make_async_remote_copy(
                    src_ref=source, dst_ref=target,
                    send_sem=move_send.at[k], recv_sem=move_recv.at[k],
                    device_id=(at_x(dx), at_y(dy)), device_id_type=MESH,
                )
            )
    for copy in moves:
        copy.start()

    def sums_and_send(d, carry):
        way_sums(d)
        way_copy(d).start()
        return carry

    def send(d, carry):
        way_copy(d).start()
        return carry

    lax.fori_loop(early * ways, ways, sums_and_send, 0)
    lax.fori_loop(0, early * ways, send, 0)
    sat_rows[...] = jnp.broadcast_to(column_of(pair[0]), sat_rows.shape)
    inverse[...] = settle_matrix(pair[1], levels)

    length = scalars.shape[2]
    width_y = LANES // width_x
    block = lax.broadcasted_iota(jnp.int32, (2 * slab, LANES), 1) // width_y
    doubled = lambda face: jnp.concatenate([face, face], axis=0)

    def flux_x(x):
        face = doubled(faces_x[x])
        return jnp.where(face > 0, face * scalars[x], face * scalars[x + 1])

    def placed(row, t, x):
        k, q = t // width_x, t % width_x
        part = row[:, k * LANES:(k + 1) * LANES]
        return part if x == q else pltpu.roll(part, ((x - q) % width_x) * width_y, 1)

    inner = [flux_x(x) for x in range(1, width_x)]
    rows = []
    for x in range(width_x):
        here, face = scalars[x + 1], doubled(faces_y[x])
        flux_y = jnp.where(face > 0, face * here, face * pltpu.roll(here, length - 1, 1))
        row = here - (flux_y - pltpu.roll(flux_y, 1, 1))
        row = row + inner[x - 1] if x > 0 else row
        rows.append(row - inner[x] if x < width_x - 1 else row)
    edges[0] = rows[0]
    edges[1] = rows[width_x - 1]
    for t in range(n_gy):
        tile = placed(rows[1], t, 1)
        for x in range(2, width_x - 1):
            tile = jnp.where(block == x, placed(rows[x], t, x), tile)
        packed[t] = tile

    for copy in halos:
        copy.wait_recv()
    first = edges[0] + flux_x(0)
    last = edges[1] - flux_x(width_x)
    for t in range(n_gy):
        tile = jnp.where(block == 0, placed(first, t, 0), packed[t])
        packed[t] = jnp.where(block == width_x - 1, placed(last, t, width_x - 1), tile)
    turns = []
    for o in range(1, n_gy):
        peer = at_y(o)
        turns.append(
            pltpu.make_async_remote_copy(
                src_ref=packed.at[peer], dst_ref=fields.at[me_y],
                send_sem=turn_sem.at[0], recv_sem=turn_sem.at[1],
                device_id=(me_x, peer), device_id_type=MESH,
            )
        )
    for copy in turns:
        copy.start()
    fields[me_y] = packed[me_y]

    resident_rows(early, 1)
    acc = add(acc, (ahead, resident // group), 0)
    total = by_level(acc)
    for k, ref in enumerate((out_mass, out_cells, in_sums)):
        all_of(ref, move_recv.at[k]).wait()
    for d in range(ways):
        total = total + in_sums[d]
    sums[...] = total

    others = packed.at[pl.ds(0, n_gy - 1)]
    all_of(others, turn_sem.at[1]).wait()
    for copy in halos:
        copy.wait_send()
    for k, ref in enumerate((out_mass, out_cells, out_sums)):
        all_of(ref, move_send.at[k]).wait()
    all_of(others, turn_sem.at[0]).wait()


def exchange_call(n_gx, n_gy, args, levels, cut):
    vapor, mass, leave = args[0], args[6], args[10]
    slab, width_x, length = vapor.shape
    resident, moving = mass.shape[2] * mass.shape[3], leave.shape[3]
    total = resident + len(OFFSETS) * moving
    f32, i32 = jnp.float32, jnp.int32
    vmem, dma = pltpu.VMEM, pltpu.SemaphoreType.DMA
    record, staged = vmem(mass.shape[2:], f32), vmem((total, LANES), f32)
    leaving = vmem(leave.shape[2:], f32)
    return pl.pallas_call(
        functools.partial(exchange_kernel, n_gx, n_gy, levels, cut),
        out_shape=[
            vmem((n_gy, 2 * slab, LANES), f32),
            vmem((total // moving, moving, LANES), f32),
            vmem((total // moving, moving, LANES), i32),
            vmem((levels, LANES), f32),
            vmem((levels, LANES), f32),
            vmem((levels, levels), f32),
        ],
        in_specs=[pl.BlockSpec(memory_space=pltpu.HBM)] * len(args),
        out_specs=[pl.BlockSpec(memory_space=vmem)] * 6,
        scratch_shapes=[
            vmem((2, 1, levels), f32),
            vmem((width_x + 2, 2 * slab, length), f32),
            vmem((width_x + 1, slab, length), f32),
            vmem((width_x, slab, length), f32),
            record,
            vmem((1, resident), i32),
            vmem((len(OFFSETS), moving), i32),
            vmem((total, LANES), i32),
            staged, staged, staged, staged,
            vmem((n_gy, 2 * slab, LANES), f32),
            vmem((2, 2 * slab, length), f32),
            leaving, leaving, vmem(leaving.shape, i32),
            vmem((len(OFFSETS), levels, LANES), f32),
            vmem((len(OFFSETS), levels, LANES), f32),
            dma((12,)), dma((3,)), dma((3,)), dma((3,)), dma((3,)), dma((2,)),
        ],
        compiler_params=pltpu.CompilerParams(
            collective_id=0, has_side_effects=True, vmem_limit_bytes=16 * 1024 * 1024
        ),
        name="exchange",
    )(*(pltpu.with_memory_space_constraint(a, pltpu.HBM) for a in args))


def column_of(row):
    n = row.shape[1]
    i = lax.broadcasted_iota(jnp.int32, (n, n), 0)
    j = lax.broadcasted_iota(jnp.int32, (n, n), 1)
    return jnp.sum(jnp.where(i == j, row, 0.0), axis=1, keepdims=True)


def settle_matrix(fall, levels):
    keep = 1.0 / (1.0 + fall)
    logs = jnp.log(fall * keep)
    i = lax.broadcasted_iota(jnp.int32, (levels, levels), 0)
    j = lax.broadcasted_iota(jnp.int32, (levels, levels), 1)
    down = jnp.sum(jnp.where(j <= i, logs, 0.0), axis=1, keepdims=True)
    across = jnp.sum(jnp.where(i <= j, column_of(logs), 0.0), axis=0, keepdims=True)
    spread = jnp.where(j >= i, across - down, 0.0)
    return jnp.where(j >= i, column_of(keep) * jnp.exp(spread), 0.0)


def grow_kernel(
    levels, chunks, width_x,
    fields, sums, sat_rows, inverse, mass, cells,
    vapor_out, heat_out, rain_out, grown_out,
    table, vapor, heat, rain, grown, sem,
):
    moist, warm = [], []
    low = lax.broadcasted_iota(jnp.int32, (8, LANES), 0) < 4
    for k in range(0, fields.shape[0], 2):
        a, b = fields[k], fields[k + 1]
        moist.append(jnp.where(low, a, pltpu.roll(b, 4, 0)))
        warm.append(jnp.where(low, pltpu.roll(a, 4, 0), b))
    moist = jnp.concatenate(moist, axis=0)
    warm = jnp.concatenate(warm, axis=0)
    excess = moist[:levels] - sat_rows[...] * jnp.exp(SAT_SLOPE * warm[:levels])
    growth = jnp.exp(GROW_RATE * excess)
    for k in range(levels):
        table[k] = jnp.broadcast_to(growth[k:k + 1], (8, LANES))

    total = sums[...]
    condensed = total * (growth - 1.0)
    vapor[...] = jnp.concatenate([moist[:levels] - condensed, moist[levels:]], axis=0).T
    heat[...] = jnp.concatenate([warm[:levels] + LATENT_HEAT * condensed, warm[levels:]], axis=0).T
    fallen = jnp.dot(
        inverse[...], total * growth,
        precision=lax.Precision.HIGHEST, preferred_element_type=jnp.float32,
    )
    width_y = LANES // width_x
    for x in range(width_x):
        rain[:, x, :] = fallen[:, x * width_y:(x + 1) * width_y]
    copies = [
        pltpu.make_async_copy(vapor, vapor_out, sem.at[0]),
        pltpu.make_async_copy(heat, heat_out, sem.at[1]),
        pltpu.make_async_copy(rain, rain_out, sem.at[2]),
    ]
    for copy in copies:
        copy.start()

    size = mass.shape[0] // chunks

    def tile(start, t):
        rows = pl.ds(pl.multiple_of(start + t * 8, 8), 8)
        c = cells[rows, :]
        lev, col = c >> 7, c & (LANES - 1)
        got = jnp.zeros((8, LANES), jnp.float32)
        for k in range(levels):
            near = jnp.take_along_axis(table[k], col, axis=1, mode="promise_in_bounds")
            got = jnp.where(lev == k, near, got)
        grown[rows, :] = mass[rows, :] * got

    def chunk(i, carry):
        start = pl.multiple_of(i * size, 8)
        for t in range(size // 8):
            tile(start, t)
        part = pl.ds(start, size)
        pltpu.make_async_copy(grown.at[part], grown_out.at[part], sem.at[3 + i]).start()
        return carry

    lax.fori_loop(0, chunks, chunk, 0)
    for i in range(chunks):
        part = pl.ds(i * size, size)
        copies.append(pltpu.make_async_copy(grown.at[part], grown_out.at[part], sem.at[3 + i]))
    for copy in copies:
        copy.wait()


def grow_call(fields, mass, cells, sums, sat_rows, inverse, width_x, chunks=4):
    f32 = jnp.float32
    levels, total = sums.shape[0], fields.shape[0] * fields.shape[1] // 2
    shapes = [(LANES, total), (LANES, total), (levels, width_x, LANES // width_x), mass.shape]
    return pl.pallas_call(
        functools.partial(grow_kernel, levels, chunks, width_x),
        out_shape=[jax.ShapeDtypeStruct(s, f32) for s in shapes],
        in_specs=[pl.BlockSpec(memory_space=pltpu.VMEM)] * 6,
        out_specs=[pl.BlockSpec(memory_space=pltpu.HBM)] * 4,
        scratch_shapes=[pltpu.VMEM((levels, 8, LANES), f32)]
        + [pltpu.VMEM(s, f32) for s in shapes]
        + [pltpu.SemaphoreType.DMA((3 + chunks,))],
        compiler_params=pltpu.CompilerParams(vmem_limit_bytes=16 * 1024 * 1024),
        name="grow_records",
    )(fields, sums, sat_rows, inverse, mass, cells)


def local(n_gx, n_gy, vapor_ratio, potential_temp, flow_x, flow_y, sat_ref, fall_rate, *records):
    levels, width_x = sat_ref.shape[0], vapor_ratio.shape[1]
    args = (vapor_ratio, potential_temp, flow_x, flow_y, sat_ref[None], fall_rate[None]) + records
    resident = records[0].shape[2]
    cut = resident * 5 // 8
    moving = records[4].shape[3]
    blocks = lambda a: a.reshape(1, 1, resident // moving, moving, LANES)
    args = args[:6] + tuple(blocks(a) for a in args[6:9]) + args[9:]
    handed = list(exchange_call(n_gx, n_gy, args, levels, cut))
    handed[1], handed[2] = (h.reshape(-1, LANES) for h in handed[1:3])
    vapor, heat, rain, grown = grow_call(*handed, width_x)
    unfold = lambda columns: columns.reshape(width_x, LANES // width_x, -1).transpose(2, 0, 1)
    return unfold(vapor), unfold(heat), rain, grown[None, None]


def solution(mesh):
    level_rows = P("gy", "gx", None)
    owned = lambda rank: P("gx", "gy", *([None] * (rank - 2)))
    return jax.shard_map(
        functools.partial(local, mesh.shape["gx"], mesh.shape["gy"]),
        mesh=mesh,
        in_specs=(level_rows,) * 4 + (P(), P()) + tuple(owned(r) for r in (4, 4, 4, 3, 5, 5, 5, 4)),
        out_specs=(P(None, "gx", "gy"),) * 3 + (owned(4),),
        check_vma=False,
    )
```

```python
import functools

import jax
import jax.numpy as jnp
from jax import lax
from jax.experimental import pallas as pl
from jax.experimental.pallas import tpu as pltpu
from jax.sharding import PartitionSpec as P

LANES = 128
PACK = 16
SAT_SLOPE = 0.3
GROW_RATE = 0.5
LATENT_HEAT = 2.5
OFFSETS = ((-1, -1), (-1, 0), (-1, 1), (0, -1), (0, 1), (1, -1), (1, 0), (1, 1))
MESH = pl.DeviceIdType.MESH


def stage_rows(blocks, mass, weight, cells, limit, first, hi, lo, lev, col):
    lane = lax.broadcasted_iota(jnp.int32, (8, LANES), 1)

    def block(t, carry):
        for half in range(2):
            at = pl.ds(half * 8, 8)
            to = pl.ds(pl.multiple_of(first + t * 16 + half * 8, 8), 8)
            m = jnp.where(lane < limit[to, :], mass[t, at, :], 0.0)
            mass[t, at, :] = m
            p = m * weight[t, at, :]
            top = p.astype(jnp.bfloat16).astype(jnp.float32)
            c = cells[t, at, :]
            hi[to, :] = top
            lo[to, :] = p - top
            lev[to, :] = (c >> 7).astype(jnp.float32)
            col[to, :] = (c & (LANES - 1)).astype(jnp.float32)
        return carry

    lax.fori_loop(blocks[0], blocks[1], block, 0)


def add_rows(acc, groups, first, hi, lo, lev, col, n_lev, group):
    bf16 = jnp.bfloat16
    zero = jnp.zeros((PACK, LANES), bf16)
    one = jnp.ones((PACK, LANES), bf16)
    base = lax.broadcasted_iota(jnp.int32, (PACK, LANES), 0)
    marks = [(base + PACK * g).astype(jnp.float32).astype(bf16) for g in range(LANES // PACK)]

    def step(i, acc):
        left, right = [], []
        for k in range(group):
            j = first + i * group + k

            def spread(ref, j=j):
                return jnp.broadcast_to(ref[pl.ds(j, 1), :], (PACK, LANES)).astype(bf16)

            h, l, v, c = spread(hi), spread(lo), spread(lev), spread(col)
            here = [v == marks[g] for g in range(n_lev)]
            picked = [jnp.where(m, h, zero) for m in here] + [jnp.where(m, l, zero) for m in here]
            right.append(jnp.concatenate(picked, axis=0))
            left.append(jnp.concatenate([jnp.where(c == m, one, zero) for m in marks], axis=0))
        left = jnp.concatenate(left, axis=1)
        right = jnp.concatenate(right, axis=1)
        return acc + lax.dot_general(
            left, right, (((1,), (1,)), ((), ())), preferred_element_type=jnp.float32
        )

    return lax.fori_loop(groups[0], groups[1], step, acc)


def exchange_kernel(
    n_gx, n_gy, levels, cut,
    vapor, warm, flow_x, flow_y, sat, fall, mass, weight, cells, counts,
    leave_mass, leave_weight, leave_cells, leave_counts,
    fields, all_mass, all_cells, sums, sat_rows, inverse,
    pair, scalars, faces_x, faces_y, all_weight, counts_in, slots, limit, hi, lo, lev, col, packed, edges,
    out_mass, out_weight, out_cells, out_sums, in_sums,
    own_sem, halo_send, halo_recv, move_send, move_recv, turn_sem,
):
    me_x, me_y = lax.axis_index("gx"), lax.axis_index("gy")

    def at_x(step):
        return lax.rem(me_x + (step + n_gx), n_gx)

    def at_y(step):
        return lax.rem(me_y + (step + n_gy), n_gy)

    resident = mass.shape[2] * mass.shape[3]
    own_mass, own_cells = all_mass.at[pl.ds(0, mass.shape[2])], all_cells.at[pl.ds(0, mass.shape[2])]
    ways, moving = leave_mass.shape[2], leave_mass.shape[3]
    arriving = ways * moving
    width_x = vapor.shape[1]
    slab = vapor.shape[0]
    n_lev = -(-levels // PACK)
    empty = jnp.zeros((LANES, 2 * n_lev * PACK), jnp.float32)

    barrier = pltpu.get_barrier_semaphore()
    peers = [(me_x, at_y(o)) for o in range(1, n_gy)]
    peers += [(at_x(dx), at_y(dy)) for dx in (-1, 1) for dy in (-1, 0, 1)]
    for peer in peers:
        pl.semaphore_signal(barrier, inc=1, device_id=peer, device_id_type=MESH)

    leaves = [
        pltpu.make_async_copy(leave_counts.at[0, 0], slots, own_sem.at[0]),
        pltpu.make_async_copy(leave_mass.at[0, 0], out_mass, own_sem.at[1]),
        pltpu.make_async_copy(leave_weight.at[0, 0], out_weight, own_sem.at[2]),
        pltpu.make_async_copy(leave_cells.at[0, 0], out_cells, own_sem.at[3]),
    ]
    loads = []
    for x in range(width_x):
        loads += [
            pltpu.make_async_copy(vapor.at[:, x, :], scalars.at[x + 1, pl.ds(0, slab)], own_sem.at[4]),
            pltpu.make_async_copy(warm.at[:, x, :], scalars.at[x + 1, pl.ds(slab, slab)], own_sem.at[4]),
            pltpu.make_async_copy(flow_x.at[:, x, :], faces_x.at[x + 1], own_sem.at[5]),
            pltpu.make_async_copy(flow_y.at[:, x, :], faces_y.at[x], own_sem.at[6]),
        ]
    loads += [
        pltpu.make_async_copy(sat, pair.at[0], own_sem.at[7]),
        pltpu.make_async_copy(fall, pair.at[1], own_sem.at[7]),
    ]
    drops = [
        pltpu.make_async_copy(counts.at[0], counts_in, own_sem.at[8]),
        pltpu.make_async_copy(mass.at[0, 0], own_mass, own_sem.at[9]),
        pltpu.make_async_copy(weight.at[0, 0], all_weight, own_sem.at[10]),
        pltpu.make_async_copy(cells.at[0, 0], own_cells, own_sem.at[11]),
    ]

    def all_of(ref, sem):
        return pltpu.make_async_copy(ref, ref, sem)

    for copy in leaves + loads + drops:
        copy.start()

    side = 4
    away = lambda v: jnp.minimum(v, side - v)
    hops = away(lax.rem(me_y, side)) + away(me_y // side)
    spare = jnp.where(me_x < 2, 9, 0) + 4 * (side - hops) - 0
    spare += jnp.where((me_x > 1) & (me_x < n_gx - 1), 7 * lax.rem(me_x, 2), 0)
    spare = jnp.where((me_x == 2) | (me_x == n_gx - 1), spare - 4, spare)
    early = jnp.where(spare >= 13, 1, 0)
    ahead = early * jnp.clip(spare - 14, 0, 12)
    group = 16
    add = functools.partial(add_rows, hi=hi, lo=lo, lev=lev, col=col, n_lev=n_lev, group=group)

    def by_level(acc):
        total = acc.T
        return total[:levels] + total[n_lev * PACK:n_lev * PACK + levels]

    def way_sums(d):
        out_sums[d] = by_level(add(empty, (0, moving // group), resident + d * moving))

    def way_copy(d):
        cell = d + d // 4 - d // 8
        return pltpu.make_async_remote_copy(
            src_ref=out_sums.at[d], dst_ref=in_sums.at[d],
            send_sem=move_send.at[2], recv_sem=move_recv.at[2],
            device_id=(at_x(cell // 3 - 1), at_y(cell % 3 - 1)), device_id_type=MESH,
        )

    def resident_rows(lower, upper):
        blocks = (lower * (resident // 16), upper * (resident // 16))
        stage_rows(blocks, all_mass, all_weight, all_cells, limit, 0, hi, lo, lev, col)

    for copy in leaves:
        copy.wait()
    turned = slots[...].T
    for d in range(ways):
        limit[resident + d * moving:resident + (d + 1) * moving, :] = jnp.broadcast_to(
            turned[:, d:d + 1], (moving, LANES)
        )
    stage_rows((0, ways), out_mass, out_weight, out_cells, limit, resident, hi, lo, lev, col)

    def sums_ahead(d, carry):
        way_sums(d)
        return carry

    lax.fori_loop(0, early * ways, sums_ahead, 0)
    for copy in drops:
        copy.wait()
    for k in range(resident // LANES):
        row = counts_in[:, k * LANES:(k + 1) * LANES]
        turned = jnp.broadcast_to(row, (8, LANES)).T
        limit[k * LANES:(k + 1) * LANES, :] = jnp.broadcast_to(turned[:, 0:1], (LANES, LANES))
    resident_rows(0, early)
    acc = add(empty, (0, ahead), 0)

    all_of(scalars.at[pl.ds(1, width_x)], own_sem.at[4]).wait()
    all_of(faces_x.at[pl.ds(1, width_x)], own_sem.at[5]).wait()
    all_of(faces_y, own_sem.at[6]).wait()
    all_of(pair, own_sem.at[7]).wait()
    pl.semaphore_wait(barrier, len(peers))

    halos = []
    for source, step, target in (
        (scalars.at[width_x], 1, scalars.at[0]),
        (faces_x.at[width_x], 1, faces_x.at[0]),
        (scalars.at[1], -1, scalars.at[width_x + 1]),
    ):
        k = len(halos)
        halos.append(
            pltpu.make_async_remote_copy(
                src_ref=source, dst_ref=target,
                send_sem=halo_send.at[k], recv_sem=halo_recv.at[k],
                device_id=(at_x(step), me_y), device_id_type=MESH,
            )
        )
    for copy in halos:
        copy.start()

    moves = []
    for d, (dx, dy) in enumerate(OFFSETS):
        for k, (source, target) in enumerate((
            (out_mass.at[d], all_mass.at[mass.shape[2] + d]),
            (out_cells.at[d], all_cells.at[mass.shape[2] + d]),
        )):
            moves.append(
                pltpu.make_async_remote_copy(
                    src_ref=source, dst_ref=target,
                    send_sem=move_send.at[k], recv_sem=move_recv.at[k],
                    device_id=(at_x(dx), at_y(dy)), device_id_type=MESH,
                )
            )
    for copy in moves:
        copy.start()

    odd = lax.rem(me_x, 2)

    def sums_and_send(i, carry):
        d = i + odd * (ways - 1 - 2 * i)
        way_sums(d)
        way_copy(d).start()
        return carry

    def send(d, carry):
        way_copy(d).start()
        return carry

    lax.fori_loop(early * ways, ways, sums_and_send, 0)
    lax.fori_loop(0, early * ways, send, 0)
    sat_rows[...] = jnp.broadcast_to(column_of(pair[0]), sat_rows.shape)
    inverse[...] = settle_matrix(pair[1], levels)

    length = scalars.shape[2]
    width_y = LANES // width_x
    block = lax.broadcasted_iota(jnp.int32, (2 * slab, LANES), 1) // width_y
    doubled = lambda face: jnp.concatenate([face, face], axis=0)

    def flux_x(x):
        face = doubled(faces_x[x])
        return jnp.where(face > 0, face * scalars[x], face * scalars[x + 1])

    def placed(row, t, x):
        k, q = t // width_x, t % width_x
        part = row[:, k * LANES:(k + 1) * LANES]
        return part if x == q else pltpu.roll(part, ((x - q) % width_x) * width_y, 1)

    inner = [flux_x(x) for x in range(1, width_x)]
    rows = []
    for x in range(width_x):
        here, face = scalars[x + 1], doubled(faces_y[x])
        flux_y = jnp.where(face > 0, face * here, face * pltpu.roll(here, length - 1, 1))
        row = here - (flux_y - pltpu.roll(flux_y, 1, 1))
        row = row + inner[x - 1] if x > 0 else row
        rows.append(row - inner[x] if x < width_x - 1 else row)
    edges[0] = rows[0]
    edges[1] = rows[width_x - 1]
    for t in range(n_gy):
        tile = placed(rows[1], t, 1)
        for x in range(2, width_x - 1):
            tile = jnp.where(block == x, placed(rows[x], t, x), tile)
        packed[t] = tile

    for copy in halos:
        copy.wait_recv()
    first = edges[0] + flux_x(0)
    last = edges[1] - flux_x(width_x)
    for t in range(n_gy):
        tile = jnp.where(block == 0, placed(first, t, 0), packed[t])
        packed[t] = jnp.where(block == width_x - 1, placed(last, t, width_x - 1), tile)
    turns = []
    for o in range(1, n_gy):
        peer = at_y(o)
        turns.append(
            pltpu.make_async_remote_copy(
                src_ref=packed.at[peer], dst_ref=fields.at[me_y],
                send_sem=turn_sem.at[0], recv_sem=turn_sem.at[1],
                device_id=(me_x, peer), device_id_type=MESH,
            )
        )
    for copy in turns:
        copy.start()
    fields[me_y] = packed[me_y]

    resident_rows(early, 1)
    acc = add(acc, (ahead, resident // group), 0)
    total = by_level(acc)
    for k, ref in enumerate((out_mass, out_cells, in_sums)):
        all_of(ref, move_recv.at[k]).wait()
    for d in range(ways):
        total = total + in_sums[d]
    sums[...] = total

    others = packed.at[pl.ds(0, n_gy - 1)]
    all_of(others, turn_sem.at[1]).wait()
    for copy in halos:
        copy.wait_send()
    for k, ref in enumerate((out_mass, out_cells, out_sums)):
        all_of(ref, move_send.at[k]).wait()
    all_of(others, turn_sem.at[0]).wait()


def exchange_call(n_gx, n_gy, args, levels, cut):
    vapor, mass, leave = args[0], args[6], args[10]
    slab, width_x, length = vapor.shape
    resident, moving = mass.shape[2] * mass.shape[3], leave.shape[3]
    total = resident + len(OFFSETS) * moving
    f32, i32 = jnp.float32, jnp.int32
    vmem, dma = pltpu.VMEM, pltpu.SemaphoreType.DMA
    record, staged = vmem(mass.shape[2:], f32), vmem((total, LANES), f32)
    leaving = vmem(leave.shape[2:], f32)
    return pl.pallas_call(
        functools.partial(exchange_kernel, n_gx, n_gy, levels, cut),
        out_shape=[
            vmem((n_gy, 2 * slab, LANES), f32),
            vmem((total // moving, moving, LANES), f32),
            vmem((total // moving, moving, LANES), i32),
            vmem((levels, LANES), f32),
            vmem((levels, LANES), f32),
            vmem((levels, levels), f32),
        ],
        in_specs=[pl.BlockSpec(memory_space=pltpu.HBM)] * len(args),
        out_specs=[pl.BlockSpec(memory_space=vmem)] * 6,
        scratch_shapes=[
            vmem((2, 1, levels), f32),
            vmem((width_x + 2, 2 * slab, length), f32),
            vmem((width_x + 1, slab, length), f32),
            vmem((width_x, slab, length), f32),
            record,
            vmem((1, resident), i32),
            vmem((len(OFFSETS), moving), i32),
            vmem((total, LANES), i32),
            staged, staged, staged, staged,
            vmem((n_gy, 2 * slab, LANES), f32),
            vmem((2, 2 * slab, length), f32),
            leaving, leaving, vmem(leaving.shape, i32),
            vmem((len(OFFSETS), levels, LANES), f32),
            vmem((len(OFFSETS), levels, LANES), f32),
            dma((12,)), dma((3,)), dma((3,)), dma((3,)), dma((3,)), dma((2,)),
        ],
        compiler_params=pltpu.CompilerParams(
            collective_id=0, has_side_effects=True, vmem_limit_bytes=16 * 1024 * 1024
        ),
        name="exchange",
    )(*(pltpu.with_memory_space_constraint(a, pltpu.HBM) for a in args))


def column_of(row):
    n = row.shape[1]
    i = lax.broadcasted_iota(jnp.int32, (n, n), 0)
    j = lax.broadcasted_iota(jnp.int32, (n, n), 1)
    return jnp.sum(jnp.where(i == j, row, 0.0), axis=1, keepdims=True)


def settle_matrix(fall, levels):
    keep = 1.0 / (1.0 + fall)
    logs = jnp.log(fall * keep)
    i = lax.broadcasted_iota(jnp.int32, (levels, levels), 0)
    j = lax.broadcasted_iota(jnp.int32, (levels, levels), 1)
    down = jnp.sum(jnp.where(j <= i, logs, 0.0), axis=1, keepdims=True)
    across = jnp.sum(jnp.where(i <= j, column_of(logs), 0.0), axis=0, keepdims=True)
    spread = jnp.where(j >= i, across - down, 0.0)
    return jnp.where(j >= i, column_of(keep) * jnp.exp(spread), 0.0)


def grow_kernel(
    levels, chunks, width_x,
    fields, sums, sat_rows, inverse, mass, cells,
    vapor_out, heat_out, rain_out, grown_out,
    table, vapor, heat, rain, grown, sem,
):
    moist, warm = [], []
    low = lax.broadcasted_iota(jnp.int32, (8, LANES), 0) < 4
    for k in range(0, fields.shape[0], 2):
        a, b = fields[k], fields[k + 1]
        moist.append(jnp.where(low, a, pltpu.roll(b, 4, 0)))
        warm.append(jnp.where(low, pltpu.roll(a, 4, 0), b))
    moist = jnp.concatenate(moist, axis=0)
    warm = jnp.concatenate(warm, axis=0)
    excess = moist[:levels] - sat_rows[...] * jnp.exp(SAT_SLOPE * warm[:levels])
    growth = jnp.exp(GROW_RATE * excess)
    for k in range(levels):
        table[k] = jnp.broadcast_to(growth[k:k + 1], (8, LANES))

    total = sums[...]
    condensed = total * (growth - 1.0)
    vapor[...] = jnp.concatenate([moist[:levels] - condensed, moist[levels:]], axis=0).T
    heat[...] = jnp.concatenate([warm[:levels] + LATENT_HEAT * condensed, warm[levels:]], axis=0).T
    fallen = jnp.dot(
        inverse[...], total * growth,
        precision=lax.Precision.HIGHEST, preferred_element_type=jnp.float32,
    )
    width_y = LANES // width_x
    for x in range(width_x):
        rain[:, x, :] = fallen[:, x * width_y:(x + 1) * width_y]
    copies = [
        pltpu.make_async_copy(vapor, vapor_out, sem.at[0]),
        pltpu.make_async_copy(heat, heat_out, sem.at[1]),
        pltpu.make_async_copy(rain, rain_out, sem.at[2]),
    ]
    for copy in copies:
        copy.start()

    size = mass.shape[0] // chunks

    def tile(start, t):
        rows = pl.ds(start + t * 8, 8)
        c = cells[rows, :]
        lev, col = c >> 7, c & (LANES - 1)
        got = jnp.zeros((8, LANES), jnp.float32)
        for k in range(levels):
            near = jnp.take_along_axis(table[k], col, axis=1, mode="promise_in_bounds")
            got = jnp.where(lev == k, near, got)
        grown[rows, :] = mass[rows, :] * got

    for i in range(chunks):
        for t in range(size // 8):
            tile(i * size, t)
        part = pl.ds(i * size, size)
        copies.append(pltpu.make_async_copy(grown.at[part], grown_out.at[part], sem.at[3 + i]))
        copies[-1].start()
    for copy in copies:
        copy.wait()


def grow_call(fields, mass, cells, sums, sat_rows, inverse, width_x, chunks=4):
    f32 = jnp.float32
    levels, total = sums.shape[0], fields.shape[0] * fields.shape[1] // 2
    shapes = [(LANES, total), (LANES, total), (levels, width_x, LANES // width_x), mass.shape]
    return pl.pallas_call(
        functools.partial(grow_kernel, levels, chunks, width_x),
        out_shape=[jax.ShapeDtypeStruct(s, f32) for s in shapes],
        in_specs=[pl.BlockSpec(memory_space=pltpu.VMEM)] * 6,
        out_specs=[pl.BlockSpec(memory_space=pltpu.HBM)] * 4,
        scratch_shapes=[pltpu.VMEM((levels, 8, LANES), f32)]
        + [pltpu.VMEM(s, f32) for s in shapes]
        + [pltpu.SemaphoreType.DMA((3 + chunks,))],
        compiler_params=pltpu.CompilerParams(vmem_limit_bytes=16 * 1024 * 1024),
        name="grow_records",
    )(fields, sums, sat_rows, inverse, mass, cells)


def local(n_gx, n_gy, vapor_ratio, potential_temp, flow_x, flow_y, sat_ref, fall_rate, *records):
    levels, width_x = sat_ref.shape[0], vapor_ratio.shape[1]
    args = (vapor_ratio, potential_temp, flow_x, flow_y, sat_ref[None], fall_rate[None]) + records
    resident = records[0].shape[2]
    cut = resident * 5 // 8
    moving = records[4].shape[3]
    blocks = lambda a: a.reshape(1, 1, resident // moving, moving, LANES)
    args = args[:6] + tuple(blocks(a) for a in args[6:9]) + args[9:]
    handed = list(exchange_call(n_gx, n_gy, args, levels, cut))
    handed[1], handed[2] = (h.reshape(-1, LANES) for h in handed[1:3])
    vapor, heat, rain, grown = grow_call(*handed, width_x)
    unfold = lambda columns: columns.reshape(width_x, LANES // width_x, -1).transpose(2, 0, 1)
    return unfold(vapor), unfold(heat), rain, grown[None, None]


def solution(mesh):
    level_rows = P("gy", "gx", None)
    owned = lambda rank: P("gx", "gy", *([None] * (rank - 2)))
    return jax.shard_map(
        functools.partial(local, mesh.shape["gx"], mesh.shape["gy"]),
        mesh=mesh,
        in_specs=(level_rows,) * 4 + (P(), P()) + tuple(owned(r) for r in (4, 4, 4, 3, 5, 5, 5, 4)),
        out_specs=(P(None, "gx", "gy"),) * 3 + (owned(4),),
        check_vma=False,
    )
```

```python
import functools

import jax
import jax.numpy as jnp
from jax import lax
from jax.experimental import pallas as pl
from jax.experimental.pallas import tpu as pltpu
from jax.sharding import PartitionSpec as P

LANES = 128
PACK = 16
SAT_SLOPE = 0.3
GROW_RATE = 0.5
LATENT_HEAT = 2.5
OFFSETS = ((-1, -1), (-1, 0), (-1, 1), (0, -1), (0, 1), (1, -1), (1, 0), (1, 1))
MESH = pl.DeviceIdType.MESH


def stage_rows(blocks, mass, weight, cells, limit, first, hi, lo, lev, col):
    lane = lax.broadcasted_iota(jnp.int32, (8, LANES), 1)

    def block(t, carry):
        for half in range(2):
            at = pl.ds(half * 8, 8)
            to = pl.ds(pl.multiple_of(first + t * 16 + half * 8, 8), 8)
            m = jnp.where(lane < limit[to, :], mass[t, at, :], 0.0)
            mass[t, at, :] = m
            p = m * weight[t, at, :]
            top = p.astype(jnp.bfloat16).astype(jnp.float32)
            c = cells[t, at, :]
            hi[to, :] = top
            lo[to, :] = p - top
            lev[to, :] = (c >> 7).astype(jnp.float32)
            col[to, :] = (c & (LANES - 1)).astype(jnp.float32)
        return carry

    lax.fori_loop(blocks[0], blocks[1], block, 0)


def add_rows(acc, groups, first, hi, lo, lev, col, n_lev, group):
    bf16 = jnp.bfloat16
    zero = jnp.zeros((PACK, LANES), bf16)
    one = jnp.ones((PACK, LANES), bf16)
    base = lax.broadcasted_iota(jnp.int32, (PACK, LANES), 0)
    marks = [(base + PACK * g).astype(jnp.float32).astype(bf16) for g in range(LANES // PACK)]

    def step(i, acc):
        left, right = [], []
        for k in range(group):
            j = first + i * group + k

            def spread(ref, j=j):
                return jnp.broadcast_to(ref[pl.ds(j, 1), :], (PACK, LANES)).astype(bf16)

            h, l, v, c = spread(hi), spread(lo), spread(lev), spread(col)
            here = [v == marks[g] for g in range(n_lev)]
            picked = [jnp.where(m, h, zero) for m in here] + [jnp.where(m, l, zero) for m in here]
            right.append(jnp.concatenate(picked, axis=0))
            left.append(jnp.concatenate([jnp.where(c == m, one, zero) for m in marks], axis=0))
        left = jnp.concatenate(left, axis=1)
        right = jnp.concatenate(right, axis=1)
        return acc + lax.dot_general(
            left, right, (((1,), (1,)), ((), ())), preferred_element_type=jnp.float32
        )

    return lax.fori_loop(groups[0], groups[1], step, acc)


def exchange_kernel(
    n_gx, n_gy, levels, cut,
    vapor, warm, flow_x, flow_y, sat, fall, mass, weight, cells, counts,
    leave_mass, leave_weight, leave_cells, leave_counts,
    fields, all_mass, all_cells, sums, sat_rows, inverse,
    pair, scalars, faces_x, faces_y, all_weight, counts_in, slots, limit, hi, lo, lev, col, packed, edges,
    out_mass, out_weight, out_cells, out_sums, in_sums,
    own_sem, halo_send, halo_recv, move_send, move_recv, turn_sem,
):
    me_x, me_y = lax.axis_index("gx"), lax.axis_index("gy")

    def at_x(step):
        return lax.rem(me_x + (step + n_gx), n_gx)

    def at_y(step):
        return lax.rem(me_y + (step + n_gy), n_gy)

    resident = mass.shape[2] * mass.shape[3]
    own_mass, own_cells = all_mass.at[pl.ds(0, mass.shape[2])], all_cells.at[pl.ds(0, mass.shape[2])]
    ways, moving = leave_mass.shape[2], leave_mass.shape[3]
    arriving = ways * moving
    width_x = vapor.shape[1]
    slab = vapor.shape[0]
    n_lev = -(-levels // PACK)
    empty = jnp.zeros((LANES, 2 * n_lev * PACK), jnp.float32)

    barrier = pltpu.get_barrier_semaphore()
    peers = [(me_x, at_y(o)) for o in range(1, n_gy)]
    peers += [(at_x(dx), at_y(dy)) for dx in (-1, 1) for dy in (-1, 0, 1)]
    for peer in peers:
        pl.semaphore_signal(barrier, inc=1, device_id=peer, device_id_type=MESH)

    leaves = [
        pltpu.make_async_copy(leave_counts.at[0, 0], slots, own_sem.at[0]),
        pltpu.make_async_copy(leave_mass.at[0, 0], out_mass, own_sem.at[1]),
        pltpu.make_async_copy(leave_weight.at[0, 0], out_weight, own_sem.at[2]),
        pltpu.make_async_copy(leave_cells.at[0, 0], out_cells, own_sem.at[3]),
    ]
    loads = []
    for x in range(width_x):
        loads += [
            pltpu.make_async_copy(vapor.at[:, x, :], scalars.at[x + 1, pl.ds(0, slab)], own_sem.at[4]),
            pltpu.make_async_copy(warm.at[:, x, :], scalars.at[x + 1, pl.ds(slab, slab)], own_sem.at[4]),
            pltpu.make_async_copy(flow_x.at[:, x, :], faces_x.at[x + 1], own_sem.at[5]),
            pltpu.make_async_copy(flow_y.at[:, x, :], faces_y.at[x], own_sem.at[6]),
        ]
    loads += [
        pltpu.make_async_copy(sat, pair.at[0], own_sem.at[7]),
        pltpu.make_async_copy(fall, pair.at[1], own_sem.at[7]),
    ]
    drops = [
        pltpu.make_async_copy(counts.at[0], counts_in, own_sem.at[8]),
        pltpu.make_async_copy(mass.at[0, 0], own_mass, own_sem.at[9]),
        pltpu.make_async_copy(weight.at[0, 0], all_weight, own_sem.at[10]),
        pltpu.make_async_copy(cells.at[0, 0], own_cells, own_sem.at[11]),
    ]

    def all_of(ref, sem):
        return pltpu.make_async_copy(ref, ref, sem)

    for copy in leaves + loads + drops:
        copy.start()

    side = 4
    away = lambda v: jnp.minimum(v, side - v)
    hops = away(lax.rem(me_y, side)) + away(me_y // side)
    spare = jnp.where(me_x < 2, 9, 0) + 4 * (side - hops) - 0
    spare += jnp.where((me_x > 1) & (me_x < n_gx - 1), 7 * lax.rem(me_x, 2), 0)
    spare = jnp.where((me_x == 2) | (me_x == n_gx - 1), spare - 4, spare)
    early = jnp.where(spare >= 13, 1, 0)
    ahead = early * jnp.clip(spare - 14, 0, 12)
    group = 16
    add = functools.partial(add_rows, hi=hi, lo=lo, lev=lev, col=col, n_lev=n_lev, group=group)

    def by_level(acc):
        total = acc.T
        return total[:levels] + total[n_lev * PACK:n_lev * PACK + levels]

    def way_sums(d):
        out_sums[d] = by_level(add(empty, (0, moving // group), resident + d * moving))

    def way_copy(d):
        cell = d + d // 4 - d // 8
        return pltpu.make_async_remote_copy(
            src_ref=out_sums.at[d], dst_ref=in_sums.at[d],
            send_sem=move_send.at[2], recv_sem=move_recv.at[2],
            device_id=(at_x(cell // 3 - 1), at_y(cell % 3 - 1)), device_id_type=MESH,
        )

    def resident_rows(lower, upper):
        blocks = (lower * (resident // 16), upper * (resident // 16))
        stage_rows(blocks, all_mass, all_weight, all_cells, limit, 0, hi, lo, lev, col)

    for copy in leaves:
        copy.wait()
    turned = slots[...].T
    for d in range(ways):
        limit[resident + d * moving:resident + (d + 1) * moving, :] = jnp.broadcast_to(
            turned[:, d:d + 1], (moving, LANES)
        )
    stage_rows((0, ways), out_mass, out_weight, out_cells, limit, resident, hi, lo, lev, col)

    def sums_ahead(d, carry):
        way_sums(d)
        return carry

    lax.fori_loop(0, early * ways, sums_ahead, 0)
    for copy in drops:
        copy.wait()
    for k in range(resident // LANES):
        row = counts_in[:, k * LANES:(k + 1) * LANES]
        turned = jnp.broadcast_to(row, (8, LANES)).T
        limit[k * LANES:(k + 1) * LANES, :] = jnp.broadcast_to(turned[:, 0:1], (LANES, LANES))
    resident_rows(0, early)
    acc = add(empty, (0, ahead), 0)

    all_of(scalars.at[pl.ds(1, width_x)], own_sem.at[4]).wait()
    all_of(faces_x.at[pl.ds(1, width_x)], own_sem.at[5]).wait()
    all_of(faces_y, own_sem.at[6]).wait()
    all_of(pair, own_sem.at[7]).wait()
    pl.semaphore_wait(barrier, len(peers))

    halos = []
    for source, step, target in (
        (scalars.at[width_x], 1, scalars.at[0]),
        (faces_x.at[width_x], 1, faces_x.at[0]),
        (scalars.at[1], -1, scalars.at[width_x + 1]),
    ):
        k = len(halos)
        halos.append(
            pltpu.make_async_remote_copy(
                src_ref=source, dst_ref=target,
                send_sem=halo_send.at[k], recv_sem=halo_recv.at[k],
                device_id=(at_x(step), me_y), device_id_type=MESH,
            )
        )
    for copy in halos:
        copy.start()

    moves = []
    for d, (dx, dy) in enumerate(OFFSETS):
        for k, (source, target) in enumerate((
            (out_mass.at[d], all_mass.at[mass.shape[2] + d]),
            (out_cells.at[d], all_cells.at[mass.shape[2] + d]),
        )):
            moves.append(
                pltpu.make_async_remote_copy(
                    src_ref=source, dst_ref=target,
                    send_sem=move_send.at[k], recv_sem=move_recv.at[k],
                    device_id=(at_x(dx), at_y(dy)), device_id_type=MESH,
                )
            )
    for copy in moves:
        copy.start()

    odd = lax.rem(me_x, 2)

    def sums_and_send(i, carry):
        d = i + odd * (ways - 1 - 2 * i)
        way_sums(d)
        way_copy(d).start()
        return carry

    def send(d, carry):
        way_copy(d).start()
        return carry

    lax.fori_loop(early * ways, ways, sums_and_send, 0)
    lax.fori_loop(0, early * ways, send, 0)
    sat_rows[...] = jnp.broadcast_to(column_of(pair[0]), sat_rows.shape)
    inverse[...] = settle_matrix(pair[1], levels)

    length = scalars.shape[2]
    width_y = LANES // width_x
    block = lax.broadcasted_iota(jnp.int32, (2 * slab, LANES), 1) // width_y
    doubled = lambda face: jnp.concatenate([face, face], axis=0)

    def flux_x(x):
        face = doubled(faces_x[x])
        return jnp.where(face > 0, face * scalars[x], face * scalars[x + 1])

    def placed(row, t, x):
        k, q = t // width_x, t % width_x
        part = row[:, k * LANES:(k + 1) * LANES]
        return part if x == q else pltpu.roll(part, ((x - q) % width_x) * width_y, 1)

    inner = [flux_x(x) for x in range(1, width_x)]
    rows = []
    for x in range(width_x):
        here, face = scalars[x + 1], doubled(faces_y[x])
        flux_y = jnp.where(face > 0, face * here, face * pltpu.roll(here, length - 1, 1))
        row = here - (flux_y - pltpu.roll(flux_y, 1, 1))
        row = row + inner[x - 1] if x > 0 else row
        rows.append(row - inner[x] if x < width_x - 1 else row)
    edges[0] = rows[0]
    edges[1] = rows[width_x - 1]
    for t in range(n_gy):
        tile = placed(rows[1], t, 1)
        for x in range(2, width_x - 1):
            tile = jnp.where(block == x, placed(rows[x], t, x), tile)
        packed[t] = tile

    for copy in halos:
        copy.wait_recv()
    first = edges[0] + flux_x(0)
    last = edges[1] - flux_x(width_x)
    for t in range(n_gy):
        tile = jnp.where(block == 0, placed(first, t, 0), packed[t])
        packed[t] = jnp.where(block == width_x - 1, placed(last, t, width_x - 1), tile)
    turns = []
    far = lambda o: min(o % 4, 4 - o % 4) + min(o // 4, 4 - o // 4)
    for o in sorted(range(1, n_gy), key=far, reverse=True):
        peer = at_y(o)
        turns.append(
            pltpu.make_async_remote_copy(
                src_ref=packed.at[peer], dst_ref=fields.at[me_y],
                send_sem=turn_sem.at[0], recv_sem=turn_sem.at[1],
                device_id=(me_x, peer), device_id_type=MESH,
            )
        )
    for copy in turns:
        copy.start()
    fields[me_y] = packed[me_y]

    resident_rows(early, 1)
    acc = add(acc, (ahead, resident // group), 0)
    total = by_level(acc)
    for k, ref in enumerate((out_mass, out_cells, in_sums)):
        all_of(ref, move_recv.at[k]).wait()
    for d in range(ways):
        total = total + in_sums[d]
    sums[...] = total

    others = packed.at[pl.ds(0, n_gy - 1)]
    all_of(others, turn_sem.at[1]).wait()
    for copy in halos:
        copy.wait_send()
    for k, ref in enumerate((out_mass, out_cells, out_sums)):
        all_of(ref, move_send.at[k]).wait()
    all_of(others, turn_sem.at[0]).wait()


def exchange_call(n_gx, n_gy, args, levels, cut):
    vapor, mass, leave = args[0], args[6], args[10]
    slab, width_x, length = vapor.shape
    resident, moving = mass.shape[2] * mass.shape[3], leave.shape[3]
    total = resident + len(OFFSETS) * moving
    f32, i32 = jnp.float32, jnp.int32
    vmem, dma = pltpu.VMEM, pltpu.SemaphoreType.DMA
    record, staged = vmem(mass.shape[2:], f32), vmem((total, LANES), f32)
    leaving = vmem(leave.shape[2:], f32)
    return pl.pallas_call(
        functools.partial(exchange_kernel, n_gx, n_gy, levels, cut),
        out_shape=[
            vmem((n_gy, 2 * slab, LANES), f32),
            vmem((total // moving, moving, LANES), f32),
            vmem((total // moving, moving, LANES), i32),
            vmem((levels, LANES), f32),
            vmem((levels, LANES), f32),
            vmem((levels, levels), f32),
        ],
        in_specs=[pl.BlockSpec(memory_space=pltpu.HBM)] * len(args),
        out_specs=[pl.BlockSpec(memory_space=vmem)] * 6,
        scratch_shapes=[
            vmem((2, 1, levels), f32),
            vmem((width_x + 2, 2 * slab, length), f32),
            vmem((width_x + 1, slab, length), f32),
            vmem((width_x, slab, length), f32),
            record,
            vmem((1, resident), i32),
            vmem((len(OFFSETS), moving), i32),
            vmem((total, LANES), i32),
            staged, staged, staged, staged,
            vmem((n_gy, 2 * slab, LANES), f32),
            vmem((2, 2 * slab, length), f32),
            leaving, leaving, vmem(leaving.shape, i32),
            vmem((len(OFFSETS), levels, LANES), f32),
            vmem((len(OFFSETS), levels, LANES), f32),
            dma((12,)), dma((3,)), dma((3,)), dma((3,)), dma((3,)), dma((2,)),
        ],
        compiler_params=pltpu.CompilerParams(
            collective_id=0, has_side_effects=True, vmem_limit_bytes=16 * 1024 * 1024
        ),
        name="exchange",
    )(*(pltpu.with_memory_space_constraint(a, pltpu.HBM) for a in args))


def column_of(row):
    n = row.shape[1]
    i = lax.broadcasted_iota(jnp.int32, (n, n), 0)
    j = lax.broadcasted_iota(jnp.int32, (n, n), 1)
    return jnp.sum(jnp.where(i == j, row, 0.0), axis=1, keepdims=True)


def settle_matrix(fall, levels):
    keep = 1.0 / (1.0 + fall)
    logs = jnp.log(fall * keep)
    i = lax.broadcasted_iota(jnp.int32, (levels, levels), 0)
    j = lax.broadcasted_iota(jnp.int32, (levels, levels), 1)
    down = jnp.sum(jnp.where(j <= i, logs, 0.0), axis=1, keepdims=True)
    across = jnp.sum(jnp.where(i <= j, column_of(logs), 0.0), axis=0, keepdims=True)
    spread = jnp.where(j >= i, across - down, 0.0)
    return jnp.where(j >= i, column_of(keep) * jnp.exp(spread), 0.0)


def grow_kernel(
    levels, chunks, width_x,
    fields, sums, sat_rows, inverse, mass, cells,
    vapor_out, heat_out, rain_out, grown_out,
    table, vapor, heat, rain, grown, sem,
):
    moist, warm = [], []
    low = lax.broadcasted_iota(jnp.int32, (8, LANES), 0) < 4
    for k in range(0, fields.shape[0], 2):
        a, b = fields[k], fields[k + 1]
        moist.append(jnp.where(low, a, pltpu.roll(b, 4, 0)))
        warm.append(jnp.where(low, pltpu.roll(a, 4, 0), b))
    moist = jnp.concatenate(moist, axis=0)
    warm = jnp.concatenate(warm, axis=0)
    excess = moist[:levels] - sat_rows[...] * jnp.exp(SAT_SLOPE * warm[:levels])
    growth = jnp.exp(GROW_RATE * excess)
    for k in range(levels):
        table[k] = jnp.broadcast_to(growth[k:k + 1], (8, LANES))

    total = sums[...]
    condensed = total * (growth - 1.0)
    vapor[...] = jnp.concatenate([moist[:levels] - condensed, moist[levels:]], axis=0).T
    heat[...] = jnp.concatenate([warm[:levels] + LATENT_HEAT * condensed, warm[levels:]], axis=0).T
    fallen = jnp.dot(
        inverse[...], total * growth,
        precision=lax.Precision.HIGHEST, preferred_element_type=jnp.float32,
    )
    width_y = LANES // width_x
    for x in range(width_x):
        rain[:, x, :] = fallen[:, x * width_y:(x + 1) * width_y]
    copies = [
        pltpu.make_async_copy(vapor, vapor_out, sem.at[0]),
        pltpu.make_async_copy(heat, heat_out, sem.at[1]),
        pltpu.make_async_copy(rain, rain_out, sem.at[2]),
    ]
    for copy in copies:
        copy.start()

    size = mass.shape[0] // chunks

    def tile(start, t):
        rows = pl.ds(start + t * 8, 8)
        c = cells[rows, :]
        lev, col = c >> 7, c & (LANES - 1)
        got = jnp.zeros((8, LANES), jnp.float32)
        for k in range(levels):
            near = jnp.take_along_axis(table[k], col, axis=1, mode="promise_in_bounds")
            got = jnp.where(lev == k, near, got)
        grown[rows, :] = mass[rows, :] * got

    for i in range(chunks):
        for t in range(size // 8):
            tile(i * size, t)
        part = pl.ds(i * size, size)
        copies.append(pltpu.make_async_copy(grown.at[part], grown_out.at[part], sem.at[3 + i]))
        copies[-1].start()
    for copy in copies:
        copy.wait()


def grow_call(fields, mass, cells, sums, sat_rows, inverse, width_x, chunks=3):
    f32 = jnp.float32
    levels, total = sums.shape[0], fields.shape[0] * fields.shape[1] // 2
    shapes = [(LANES, total), (LANES, total), (levels, width_x, LANES // width_x), mass.shape]
    return pl.pallas_call(
        functools.partial(grow_kernel, levels, chunks, width_x),
        out_shape=[jax.ShapeDtypeStruct(s, f32) for s in shapes],
        in_specs=[pl.BlockSpec(memory_space=pltpu.VMEM)] * 6,
        out_specs=[pl.BlockSpec(memory_space=pltpu.HBM)] * 4,
        scratch_shapes=[pltpu.VMEM((levels, 8, LANES), f32)]
        + [pltpu.VMEM(s, f32) for s in shapes]
        + [pltpu.SemaphoreType.DMA((3 + chunks,))],
        compiler_params=pltpu.CompilerParams(vmem_limit_bytes=16 * 1024 * 1024),
        name="grow_records",
    )(fields, sums, sat_rows, inverse, mass, cells)


def local(n_gx, n_gy, vapor_ratio, potential_temp, flow_x, flow_y, sat_ref, fall_rate, *records):
    levels, width_x = sat_ref.shape[0], vapor_ratio.shape[1]
    args = (vapor_ratio, potential_temp, flow_x, flow_y, sat_ref[None], fall_rate[None]) + records
    resident = records[0].shape[2]
    cut = resident * 5 // 8
    moving = records[4].shape[3]
    blocks = lambda a: a.reshape(1, 1, resident // moving, moving, LANES)
    args = args[:6] + tuple(blocks(a) for a in args[6:9]) + args[9:]
    handed = list(exchange_call(n_gx, n_gy, args, levels, cut))
    handed[1], handed[2] = (h.reshape(-1, LANES) for h in handed[1:3])
    vapor, heat, rain, grown = grow_call(*handed, width_x)
    unfold = lambda columns: columns.reshape(width_x, LANES // width_x, -1).transpose(2, 0, 1)
    return unfold(vapor), unfold(heat), rain, grown[None, None]


def solution(mesh):
    level_rows = P("gy", "gx", None)
    owned = lambda rank: P("gx", "gy", *([None] * (rank - 2)))
    return jax.shard_map(
        functools.partial(local, mesh.shape["gx"], mesh.shape["gy"]),
        mesh=mesh,
        in_specs=(level_rows,) * 4 + (P(), P()) + tuple(owned(r) for r in (4, 4, 4, 3, 5, 5, 5, 4)),
        out_specs=(P(None, "gx", "gy"),) * 3 + (owned(4),),
        check_vma=False,
    )
```
